32 devices in a mesh: groups: 2 (over y), prow: 4 (over x, core), pcol: 4 (over z).
Axes of the slice: x: 2, y: 2, z: 4, core: 2. Of those that a mesh axis runs over, the one named last changes fastest.
Arguments:
- anc_inverse: float32 [4096, 2048], P(('groups', 'prow'), 'pcol'), parts along dimension 0
- anc_factor: float32 [8, 2048, 256], P('groups', ('prow', 'pcol')), parts along dimension 0, may hold values from -0.0625 to 0.0625
- win_factor: float32 [12, 256, 256], P('groups'), parts along dimension 0, may hold values from -0.1875 to 0.1875
- diag_inverse: float32 [8, 256, 256], P('groups'), parts along dimension 0
- first_reader: int32 [32], P('groups'), parts along dimension 0, may hold values from 0 to 4
Outputs:
- anc_panels: float32 [8, 2048, 256], P('groups', ('prow', 'pcol')), parts along dimension 0
- window_inverse: float32 [8, 4, 256, 256], P('groups'), parts along dimension 0
The draws below stay inside these ranges and needn't reach their ends.
There are 2 independent parts, one for each index of `groups`. The reference program is written for one: setup_inputs(seed, part) draws one part's arguments, and reference() takes and returns one part's arrays. A program takes and returns all parts, laid end to end along the dimension named above; each array names one. Nothing has to cross between parts.
Inputs may be any that keep to these rules, and one draw needn't show every extreme that they name: Ancestor block b belongs to the pattern of supernode k exactly when first_reader[b] <= k; the value 4 puts it in no pattern, so patterns grow with k. Within each part, anc_inverse is symmetric: anc_inverse[r, s] = anc_inverse[s, r].
All inputs are finite; a program needn't handle non-finite values.
Results may differ from the reference program's by a relative error of at most 0.0003.
Values sent between devices are 32-bit elements; how exact they have to be, the bound alone decides.
A program may use at most 64 MiB of HBM per device.

```python
import math
import jax
import jax.numpy as jnp
from jax import lax

W = 256
K = 4
BLK = 128
S = 2048
SB = 16
PAIRS = 6


def draw_anc_inverse(key, part):
    key_noise, key_scale, key_diag = jax.random.split(key, 3)
    noise = jax.random.normal(key_noise, (S, S), jnp.float32)
    scales = jnp.exp(jax.random.uniform(key_scale, (S,), jnp.float32, 0.0, math.log(10.0)))
    symmetric = (noise + noise.T) * (0.5 / math.sqrt(S))
    diagonal = jax.random.uniform(key_diag, (S,), jnp.float32, 1.0, 4.0)
    sides = jnp.sqrt(scales)
    return symmetric * sides[:, None] * sides[None, :] + jnp.diag(diagonal * scales)


def draw_diag_inverse(key, part):
    key_lower, key_diag = jax.random.split(key, 2)
    lower = jax.random.normal(key_lower, (K, W, W), jnp.float32) * (0.6 / math.sqrt(W))
    diagonal = jax.random.uniform(key_diag, (K, W), jnp.float32, 0.5, 1.5)
    identity = jnp.eye(W, dtype=jnp.float32)
    return jnp.tril(lower, -1) + identity[None, :, :] * diagonal[:, :, None]


def set_ends(result, key, least, largest):
    longest = result.shape.index(max(result.shape))
    spots = []
    for shift in (0, 1):
        where = [jax.random.randint(jax.random.fold_in(key, axis), (), 0, length) for axis, length in enumerate(result.shape)]
        where[longest] = (where[longest] + shift) % result.shape[longest]
        spots.append(tuple(where))
    return result.at[spots[0]].set(least).at[spots[1]].set(largest)


def level_of(own_key, shape, cuts, least, top_value):
    loudness, own = 1.0, jax.random.fold_in(own_key, 6)
    for axis_at, parts in cuts:
        draws = jnp.exp(jax.random.uniform(jax.random.fold_in(own, axis_at), (parts,), jnp.float32, least / len(cuts), top_value / len(cuts)))
        loudness = loudness * jnp.repeat(draws, shape[axis_at] // parts).reshape([-1 if axis == axis_at else 1 for axis in range(len(shape))])
    return loudness


def centred(own_key, extent, spread, limit, cuts=(), kind=jnp.bfloat16):
    drawn = spread * jax.random.normal(own_key, extent, jnp.float32)
    if cuts:
        drawn = drawn * level_of(own_key, extent, cuts, -0.22, 0.18)
    return jnp.clip(drawn, -limit, limit).astype(kind)


def setup_inputs(seed: int = 0, part: int = 0) -> dict:
    arg_keys = jax.random.split(jax.random.key(seed), 6)
    part_splits = jax.random.split(jax.random.fold_in(arg_keys[5], part), 6)
    anc_inverse = draw_anc_inverse(jax.random.fold_in(jax.random.fold_in(arg_keys[5], part), 71), part)
    anc_factor = centred(part_splits[1], (K, S, W), (4 * S) ** -0.5, 0.0625, ((1, 16),), jnp.float32)
    win_factor = centred(part_splits[2], (PAIRS, W, W), (K * W) ** -0.5, 0.1875, (), jnp.float32)
    diag_inverse = draw_diag_inverse(jax.random.fold_in(jax.random.fold_in(arg_keys[5], part), 71), part)
    first_reader = set_ends(jax.random.randint(part_splits[4], (SB,), 0, K + 1), jax.random.fold_in(part_splits[4], 1), 0, K).astype(jnp.int32)
    return dict(anc_inverse=anc_inverse, anc_factor=anc_factor, win_factor=win_factor, diag_inverse=diag_inverse, first_reader=first_reader)


def reference(anc_inverse, anc_factor, win_factor, diag_inverse, first_reader):
    highest = lax.Precision.HIGHEST
    block_of = jnp.arange(S, dtype=jnp.int32) // BLK
    readers = first_reader[block_of]
    panels = [None] * K
    blocks = [[None] * K for column in range(K)]
    for node in reversed(range(K)):
        row_mask = (readers <= node).astype(jnp.float32)[:, None]
        linv = diag_inverse[node]
        later = list(range(node + 1, K))
        lower_u = jnp.dot(anc_factor[node], linv, precision=highest) * row_mask
        upper_u = {}
        for other in later:
            upper_u[other] = jnp.dot(win_factor[other * (other - 1) // 2 + node], linv, precision=highest)
        full_x = jnp.dot(anc_inverse, lower_u, precision=highest)
        for other in later:
            full_x = full_x + jnp.dot(panels[other], upper_u[other], precision=highest)
        cross = {}
        for other in later:
            term = jnp.dot(panels[other].T, lower_u, precision=highest)
            for second in later:
                term = term + jnp.dot(blocks[other][second], upper_u[second], precision=highest)
            cross[other] = term
        panels[node] = -full_x * row_mask
        own = jnp.dot(linv.T, linv, precision=highest) + jnp.dot(lower_u.T, full_x, precision=highest)
        for other in later:
            own = own + jnp.dot(upper_u[other].T, cross[other], precision=highest)
        blocks[node][node] = own
        for other in later:
            blocks[other][node] = -cross[other]
            blocks[node][other] = -cross[other].T
    anc_panels = jnp.stack(panels)
    window_inverse = jnp.stack([jnp.stack(blocks[row_at]) for row_at in range(K)])
    return anc_panels, window_inverse
```

```python
import functools

import jax
import jax.numpy as jnp
from jax import lax
from jax.experimental import pallas as pl
from jax.experimental.pallas import tpu as pltpu
from jax.sharding import PartitionSpec as P

BLK = 128
PIECES = 4
ACROSS = 2
MESH = pl.DeviceIdType.MESH


def split(x):
    high = x.astype(jnp.bfloat16)
    return high, (x - high.astype(jnp.float32)).astype(jnp.bfloat16)


def product(a, b):
    dot = functools.partial(jnp.dot, preferred_element_type=jnp.float32)
    return dot(a[0], b[0]) + (dot(a[0], b[1]) + dot(a[1], b[0]))


def pair_at(first, second):
    return second * (second + 1) // 2 + first


def log2(n):
    return n.bit_length() - 1


class Plan:
    def __init__(self, n_prow, n_pcol, count, width):
        self.levels = [("prow", b) for b in range(log2(n_prow))] + [("pcol", b) for b in range(log2(n_pcol))]
        self.size = [(node + 1) * width for node in range(count)]
        self.base = [pair_at(0, node) * width for node in range(count)]
        self.halvings = []
        for node in range(count):
            h = 0
            while h < len(self.levels) - 1 and self.size[node] // 2 ** (h + 1) % 8 == 0:
                h += 1
            self.halvings.append(h)
        self.piece = [self.size[node] // 2 ** self.halvings[node] for node in range(count)]
        self.piece_base = [sum(self.piece[:node]) for node in range(count)]
        self.half_base = []
        self.half_rows = []
        for level in range(len(self.levels)):
            at, bases = 0, []
            for node in range(count):
                bases.append(at)
                if level < self.halvings[node]:
                    at += self.size[node] // 2 ** (level + 1)
            self.half_base.append(bases)
            self.half_rows.append(max(at, 8))
        self.full = max(len(self.levels) - h for h in self.halvings)
        self.rows = sum(self.size)


def kernel(
    n_prow, n_pcol, plan, readers_ref, a_hbm, f_hbm, win_hbm, diag_hbm, panels_hbm, pairs_hbm,
    a_ref, f_ref, win_ref, diag_ref, v_ref, ah_ref, al_ref, ath_ref, atl_ref, vh_ref, vl_ref,
    wh_ref, wl_ref, dh_ref, dl_ref, x_ref, s_ref, panel_ref,
    whole_ref, part_ref, inbox_ref, line_ref, turn_ref, y_ref, sum_ref, final_ref, full_in, full_tmp,
    load_sem, out_sem, g1_send, g1_recv, g2_send, g2_recv, rs_send, rs_recv,
    line_send, line_recv, turn_send, turn_recv, y_send, y_recv, w_send, w_recv, back_send, back_recv,
    *more_refs,
):
    loads = [
        pltpu.make_async_copy(source, target, load_sem.at[at])
        for at, (source, target) in enumerate(
            [(f_hbm, f_ref), (a_hbm, a_ref), (diag_hbm, diag_ref), (win_hbm, win_ref)]
        )
    ]
    for load in loads:
        load.start()
    count, fine, width = f_ref.shape
    per_column = n_prow // n_pcol
    step = n_prow // PIECES
    quarter = fine // PIECES
    bits = log2(n_prow)
    turn_in = more_refs[:bits]
    half_refs = more_refs[bits:]
    p = lax.axis_index("prow")
    z = lax.axis_index("pcol")
    order = list(reversed(range(count)))
    across = order[:ACROSS]
    along = order[ACROSS:]

    barrier = pltpu.get_barrier_semaphore()

    def greet(at, carry):
        row, col = at // n_pcol, at % n_pcol

        @pl.when(at != p * n_pcol + z)
        def _():
            pl.semaphore_signal(barrier, inc=1, device_id={"prow": row, "pcol": col}, device_id_type=MESH)

        return carry

    lax.fori_loop(0, n_prow * n_pcol, greet, 0)

    reader = readers_ref[(p * n_pcol + z) * fine // BLK]
    masks = [jnp.where(reader <= node, 1.0, 0.0).astype(jnp.float32) for node in range(count)]

    def rows(start, size):
        return pl.ds(start if isinstance(start, int) else pl.multiple_of(start, 8), size)

    share = v_ref.shape[1] - fine
    unit_row = lax.broadcasted_iota(jnp.int32, (share, width), 0) + (p * n_pcol + z) * share
    unit_col = lax.broadcasted_iota(jnp.int32, (share, width), 1)

    def win_at(first, second):
        at = second * (second - 1) // 2 + first
        return wh_ref[at], wl_ref[at]

    def diag_at(node):
        return dh_ref[node], dl_ref[node]

    def split_factors():
        loads[2].wait()
        loads[3].wait()
        for node in range(count):
            dh_ref[node], dl_ref[node] = split(diag_ref[node])
        for at in range(win_ref.shape[0]):
            wh_ref[at], wl_ref[at] = split(win_ref[at])

    def local_v(node):
        units = jnp.where(unit_row == unit_col + node * width, 1.0, 0.0).astype(jnp.float32)
        total = jnp.concatenate([f_ref[node], units], axis=0)
        for other in range(node + 1, count):
            total = total - product(split(v_ref[other]), win_at(node, other))
        v = product(split(total), diag_at(node))
        v_ref[node] = v
        vh_ref[node], vl_ref[node] = split(v.T)

    def before_x(node):
        total = jnp.zeros((fine, width), jnp.float32)
        for other in range(node + 1, count):
            total = total + product(split(x_ref[other]), win_at(node, other))
        s_ref[node] = total

    def panel_copy(node):
        return pltpu.make_async_copy(panel_ref.at[node], panels_hbm.at[node], out_sem.at[0, node])

    def window_part(node, y):
        x = product(split(y - s_ref[node]), diag_at(node))
        x_ref[node] = x
        ends = split(jnp.concatenate([x, v_ref[node, pl.ds(fine, share)]], axis=0))
        for other in range(node + 1):
            sum_ref[pl.ds(pair_at(other, node) * width, width)] = product((vh_ref[other], vl_ref[other]), ends)
        panel_ref[node] = -x * masks[node]
        panel_copy(node).start()

    source = (p % per_column) * n_pcol + z
    column = p // per_column

    def g1_copy(node, q):
        return pltpu.make_async_remote_copy(
            src_ref=f_ref.at[node, pl.ds(q * quarter, quarter)],
            dst_ref=whole_ref.at[node - len(along), source, q],
            send_sem=g1_send.at[node, q],
            recv_sem=g1_recv.at[node],
            device_id={"prow": q * step, "pcol": column},
            device_id_type=MESH,
        )

    def g1_start(node):
        for q in range(PIECES):
            mine = jnp.logical_and(p == q * step, z == column)

            @pl.when(mine)
            def _():
                pltpu.make_async_copy(
                    f_ref.at[node, pl.ds(q * quarter, quarter)],
                    whole_ref.at[node - len(along), source, q],
                    g1_recv.at[node],
                ).start()

            @pl.when(jnp.logical_not(mine))
            def _():
                g1_copy(node, q).start()

    def g1_finish(node):
        for q in range(PIECES):
            mine = jnp.logical_and(p == q * step, z == column)

            @pl.when(jnp.logical_not(mine))
            def _():
                g1_copy(node, q).wait_send()

    def g2_copy(node, q, row):
        return pltpu.make_async_remote_copy(
            src_ref=whole_ref.at[node - len(along), :, q],
            dst_ref=whole_ref.at[node - len(along), :, q],
            send_sem=g2_send.at[node, row],
            recv_sem=g2_recv.at[node, q],
            device_id={"prow": row, "pcol": z},
            device_id_type=MESH,
        )

    def g2_start(node):
        for q in range(PIECES):
            @pl.when(p == q * step)
            def _():
                held = whole_ref.at[node - len(along), :, q]
                pltpu.make_async_copy(held, held, g1_recv.at[node]).wait()
                for row in range(n_prow):
                    if row != q * step:
                        g2_copy(node, q, row).start()

    def g2_wait(node):
        for q in range(PIECES):
            @pl.when(p != q * step)
            def _():
                g2_copy(node, q, 0).wait_recv()

    def g2_finish(node):
        for q in range(PIECES):
            @pl.when(p == q * step)
            def _():
                for row in range(n_prow):
                    if row != q * step:
                        g2_copy(node, q, row).wait_send()

    def rs_copy(node, side, dest):
        return pltpu.make_async_remote_copy(
            src_ref=part_ref.at[node - len(along), dest],
            dst_ref=inbox_ref.at[node - len(along), side, dest],
            send_sem=rs_send.at[node, dest],
            recv_sem=rs_recv.at[node, side, dest],
            device_id={"prow": p, "pcol": z + 1 if side == 0 else z - 1},
            device_id_type=MESH,
        )

    def rs_steps(node, relayed):
        at = node - len(along)
        for far in range(1, n_pcol):
            for side in (0, 1):
                dest = n_pcol - far if side == 0 else far - 1
                first = z == (0 if side == 0 else n_pcol - 1)
                before = z < dest if side == 0 else z > dest
                if relayed:
                    @pl.when(jnp.logical_and(before, jnp.logical_not(first)))
                    def _():
                        rs_copy(node, side, dest).wait_recv()
                        part_ref[at, dest] += inbox_ref[at, side, dest]
                        rs_copy(node, side, dest).start()
                else:
                    @pl.when(jnp.logical_and(before, first))
                    def _():
                        rs_copy(node, side, dest).start()

    def rs_end(node):
        at = node - len(along)
        for dest in range(n_pcol):
            @pl.when(z == dest)
            def _():
                total = part_ref[at, dest]
                if dest > 0:
                    rs_copy(node, 0, dest).wait_recv()
                    total = total + inbox_ref[at, 0, dest]
                if dest < n_pcol - 1:
                    rs_copy(node, 1, dest).wait_recv()
                    total = total + inbox_ref[at, 1, dest]
                part_ref[at, dest] = total
        return part_ref[at, z]

    def rs_finish(node):
        for dest in range(n_pcol):
            @pl.when(z != dest)
            def _():
                rs_copy(node, 0, dest).wait_send()

    def split_a():
        loads[1].wait()
        ah_ref[...], al_ref[...] = split(a_ref[...])

    def multiply(node):
        at = node - len(along)
        gathered = whole_ref[at].reshape(a_ref.shape[1], width)
        result = product((ah_ref[...], al_ref[...]), split(gathered))
        part_ref[at] = result.reshape(n_pcol, fine, width)

    def line_copy(node, side, hop):
        origin = z - hop if side == 0 else z + hop
        return pltpu.make_async_remote_copy(
            src_ref=line_ref.at[node, origin],
            dst_ref=line_ref.at[node, origin],
            send_sem=line_send.at[node, side, hop],
            recv_sem=line_recv.at[node, side, hop],
            device_id={"prow": p, "pcol": z + 1 if side == 0 else z - 1},
            device_id_type=MESH,
        )

    def line_sends(side, hop):
        if side == 0:
            return jnp.logical_and(z >= hop, z < n_pcol - 1)
        return jnp.logical_and(z + hop < n_pcol, z > 0)

    def line_gets(side, hop):
        return z - 1 - hop >= 0 if side == 0 else z + 1 + hop < n_pcol

    def line_wait(node, hop):
        for side in (0, 1):
            @pl.when(line_gets(side, hop))
            def _():
                origin = z - 1 - hop if side == 0 else z + 1 + hop
                pltpu.make_async_remote_copy(
                    src_ref=line_ref.at[node, origin],
                    dst_ref=line_ref.at[node, origin],
                    send_sem=line_send.at[node, side, hop],
                    recv_sem=line_recv.at[node, side, hop],
                    device_id={"prow": p, "pcol": z - 1 if side == 0 else z + 1},
                    device_id_type=MESH,
                ).wait_recv()

    def line_step(node, hop):
        if hop > 0:
            line_wait(node, hop - 1)
        if hop < n_pcol - 1:
            for side in (0, 1):
                @pl.when(line_sends(side, hop))
                def _():
                    line_copy(node, side, hop).start()

    def line_finish(node):
        for hop in range(n_pcol - 1):
            for side in (0, 1):
                @pl.when(line_sends(side, hop))
                def _():
                    line_copy(node, side, hop).wait_send()

    def split_turned():
        turned = split(a_ref[...].T)
        for group in range(n_prow // PIECES):
            for owner in range(PIECES):
                for chunk in range(PIECES):
                    at = (group * PIECES + owner) * fine + chunk * quarter
                    to = (group * PIECES + chunk) * fine + owner * quarter
                    ath_ref[pl.ds(to, quarter)] = turned[0][at : at + quarter]
                    atl_ref[pl.ds(to, quarter)] = turned[1][at : at + quarter]

    turn_starts = [0]
    for bit in range(bits):
        turn_starts.append(turn_starts[bit] + (p // 2**bit) % 2 * (n_prow // 2 ** (bit + 1)))
    slot = turn_starts[bits]

    def mate(axis, bit):
        if axis == "prow":
            return {"prow": p + (1 - (p // 2**bit) % 2 * 2) * 2**bit, "pcol": z}
        return {"prow": p, "pcol": z + (1 - (z // 2**bit) % 2 * 2) * 2**bit}

    def turn_copy(node, bit):
        half = n_prow // 2 ** (bit + 1)
        away = turn_starts[bit] + (1 - (p // 2**bit) % 2) * half
        return pltpu.make_async_remote_copy(
            src_ref=turn_ref.at[node, pl.ds(away, half)],
            dst_ref=turn_in[bit].at[node],
            send_sem=turn_send.at[node, bit],
            recv_sem=turn_recv.at[node, bit],
            device_id=mate("prow", bit),
            device_id_type=MESH,
        )

    def turn_multiply(node):
        gathered = line_ref[node].reshape(a_ref.shape[0], width)
        result = product((ath_ref[...], atl_ref[...]), split(gathered))
        turn_ref[node] = result.reshape(n_prow, PIECES, quarter, width)
        turn_copy(node, 0).start()

    def y_copy(node, owner):
        place = slot // PIECES * PIECES + owner
        return pltpu.make_async_remote_copy(
            src_ref=turn_ref.at[node, slot, owner],
            dst_ref=y_ref.at[node, slot % PIECES],
            send_sem=y_send.at[node, owner],
            recv_sem=y_recv.at[node],
            device_id={"prow": z * per_column + place // n_pcol, "pcol": place % n_pcol},
            device_id_type=MESH,
        )

    def y_mine(owner):
        place = slot // PIECES * PIECES + owner
        return jnp.logical_and(z * per_column + place // n_pcol == p, place % n_pcol == z)

    def turn_step(node, bit):
        turn_copy(node, bit).wait_recv()
        mine = pl.ds(turn_starts[bit + 1], n_prow // 2 ** (bit + 1))
        turn_ref[node, mine] += turn_in[bit][node]
        if bit + 1 < bits:
            turn_copy(node, bit + 1).start()
            return
        for owner in range(PIECES):
            @pl.when(y_mine(owner))
            def _():
                pltpu.make_async_copy(
                    turn_ref.at[node, slot, owner], y_ref.at[node, slot % PIECES], y_recv.at[node]
                ).start()

            @pl.when(jnp.logical_not(y_mine(owner)))
            def _():
                y_copy(node, owner).start()

    def y_end(node):
        pltpu.make_async_copy(y_ref.at[node], y_ref.at[node], y_recv.at[node]).wait()
        return y_ref[node].reshape(fine, width)

    def turn_finish(node):
        for bit in range(bits):
            turn_copy(node, bit).wait_send()
        for owner in range(PIECES):
            @pl.when(jnp.logical_not(y_mine(owner)))
            def _():
                y_copy(node, owner).wait_send()

    levels = plan.levels

    def level_bit(level):
        axis, bit = levels[level]
        return ((p if axis == "prow" else z) // 2**bit) % 2

    offsets = []
    for node in range(count):
        starts = [0]
        for level in range(plan.halvings[node]):
            starts.append(starts[level] + level_bit(level) * (plan.size[node] // 2 ** (level + 1)))
        offsets.append(starts)

    def piece_rows(node):
        return rows(plan.base[node] + offsets[node][plan.halvings[node]], plan.piece[node])

    def full_rows(node):
        return pl.ds(plan.piece_base[node], plan.piece[node])

    def half_rows(node, level):
        return pl.ds(plan.half_base[level][node], plan.size[node] // 2 ** (level + 1))

    def w_copy(node, level):
        h = plan.halvings[node]
        if level < h:
            half = plan.size[node] // 2 ** (level + 1)
            away = plan.base[node] + offsets[node][level] + (1 - level_bit(level)) * half
            source_ref = sum_ref.at[rows(away, half)]
            target_ref = half_refs[level].at[half_rows(node, level)]
        else:
            if level == h:
                source_ref = sum_ref.at[piece_rows(node)]
            else:
                source_ref = full_tmp.at[level - h - 1, full_rows(node)]
            target_ref = full_in.at[level - h, full_rows(node)]
        return pltpu.make_async_remote_copy(
            src_ref=source_ref,
            dst_ref=target_ref,
            send_sem=w_send.at[node, level],
            recv_sem=w_recv.at[node, level],
            device_id=mate(*levels[level]),
            device_id_type=MESH,
        )

    def w_end(node, level):
        h = plan.halvings[node]
        w_copy(node, level).wait_recv()
        if level < h:
            mine = rows(plan.base[node] + offsets[node][level + 1], plan.size[node] // 2 ** (level + 1))
            sum_ref[mine] += half_refs[level][half_rows(node, level)]
            return
        held = sum_ref[piece_rows(node)] if level == h else full_tmp[level - h - 1, full_rows(node)]
        total = held + full_in[level - h, full_rows(node)]
        if level == len(levels) - 1:
            final_ref[piece_rows(node)] = total
        else:
            full_tmp[level - h, full_rows(node)] = total

    def back_copy(node, level):
        part = rows(plan.base[node] + offsets[node][level + 1], plan.size[node] // 2 ** (level + 1))
        return pltpu.make_async_remote_copy(
            src_ref=final_ref.at[part],
            dst_ref=final_ref.at[part],
            send_sem=back_send.at[node, level],
            recv_sem=back_recv.at[node, level],
            device_id=mate(*levels[level]),
            device_id_type=MESH,
        )

    def pairs_copy(node):
        part = pl.ds(plan.base[node], plan.size[node])
        return pltpu.make_async_copy(final_ref.at[part], pairs_hbm.at[part], out_sem.at[1, node])

    def window_steps(node):
        h = plan.halvings[node]
        steps = []
        for level in range(len(levels)):
            def run(level=level):
                w_end(node, level)
                if level + 1 < len(levels):
                    w_copy(node, level + 1).start()
                else:
                    back_copy(node, h - 1).start()
            steps.append(run)
        for level in reversed(range(h)):
            def run(level=level):
                back_copy(node, level).wait_recv()
                if level > 0:
                    back_copy(node, level - 1).start()
                else:
                    pairs_copy(node).start()
            steps.append(run)
        return steps

    def close(node, end):
        window_part(node, end(node))
        w_copy(node, 0).start()

    due = []

    def at(time, run, *args):
        due.append((time, len(due), functools.partial(run, *args)))

    hops = n_pcol - 1
    at(0.5, split_a)
    at(3.0, split_factors)
    at(2.0, split_turned)
    for turn, node in enumerate(order):
        at(5.0 + turn, local_v, node)
    ends = {}
    for turn, node in enumerate(across):
        start = 2.5 * turn
        at(0.1 * turn, g1_start, node)
        at(4.5 + start, g2_start, node)
        at(10 + start, g2_wait, node)
        at(10 + start, multiply, node)
        at(10.1 + start, rs_steps, node, False)
        at(14 + start, rs_steps, node, True)
        ends[node] = 20 + start
    for turn, node in enumerate(along):
        start = 5.0 * turn
        at(1.0 + start, line_step, node, 0)
        for hop in range(1, hops + 1):
            at(1.0 + start + 5.0 * hop, line_step, node, hop)
        done = 1.1 + start + 5.0 * hops
        at(done, turn_multiply, node)
        for bit in range(bits):
            done += 2.0 if bit == 0 else 5.0
            at(done, turn_step, node, bit)
        ends[node] = max(done + 5.0, ends[node + 1] + 4.0)
    for node in order:
        end = ends[node]
        at(end - 1.0, before_x, node)
        at(end, close, node, rs_end if node in across else y_end)
        steps = window_steps(node)
        for level, run in enumerate(steps):
            end += 2.0 if level in (0, len(steps) - 1) else 5.0
            at(end, run)

    loads[0].wait()
    for node in range(count):
        f_ref[node] = f_ref[node] * masks[node]
    for node in along:
        line_ref[node, z] = f_ref[node]
    pl.semaphore_wait(barrier, n_prow * n_pcol - 1)
    for _, _, run in sorted(due, key=lambda entry: entry[:2]):
        run()
    for node in across:
        g1_finish(node)
        g2_finish(node)
        rs_finish(node)
    for node in along:
        line_finish(node)
        turn_finish(node)
    for node in order:
        for level in range(len(levels)):
            w_copy(node, level).wait_send()
        for level in range(plan.halvings[node]):
            back_copy(node, level).wait_send()
        panel_copy(node).wait()
        pairs_copy(node).wait()


def assemble_kernel(panels_in, pairs_in, panels_out, window_out, panel_ref, pairs_ref, turned_ref, in_sem, out_sem):
    count, _, width = panels_in.shape
    into = pltpu.make_async_copy(panels_in, panel_ref, in_sem.at[0])
    into.start()
    order = [(first, second) for second in reversed(range(count)) for first in range(second + 1)]

    def load(first, second):
        at = pair_at(first, second)
        return pltpu.make_async_copy(pairs_in.at[pl.ds(at * width, width)], pairs_ref.at[at], in_sem.at[1 + at])

    for first, second in order:
        load(first, second).start()
    stores = []
    for first, second in order:
        at = pair_at(first, second)
        load(first, second).wait()
        stores.append(pltpu.make_async_copy(pairs_ref.at[at], window_out.at[first, second], out_sem.at[1 + len(stores)]))
        stores[-1].start()
        if first != second:
            turned_ref[at] = pairs_ref[at].T
            stores.append(
                pltpu.make_async_copy(turned_ref.at[at], window_out.at[second, first], out_sem.at[1 + len(stores)])
            )
            stores[-1].start()
    into.wait()
    stores.append(pltpu.make_async_copy(panel_ref, panels_out, out_sem.at[0]))
    stores[-1].start()
    for store in stores:
        store.wait()


def sweep(n_prow, n_pcol, readers, anc_inverse, anc_factor, win_factor, diag_inverse):
    count, fine, width = anc_factor.shape
    pairs = count * (count + 1) // 2
    share = count * width // (n_prow * n_pcol)
    bits = log2(n_prow)
    quarter = fine // PIECES
    along = count - ACROSS
    plan = Plan(n_prow, n_pcol, count, width)
    levels = len(plan.levels)
    block_rows, block_cols = anc_inverse.shape
    hbm = pl.BlockSpec(memory_space=pltpu.HBM)
    operands = (anc_inverse, anc_factor, win_factor, diag_inverse)
    f32, b16 = jnp.float32, jnp.bfloat16
    dma = pltpu.SemaphoreType.DMA
    panels, blocks = pl.pallas_call(
        functools.partial(kernel, n_prow, n_pcol, plan),
        out_shape=(
            jax.ShapeDtypeStruct((count, fine, width), f32),
            jax.ShapeDtypeStruct((pairs * width, width), f32),
        ),
        in_specs=[pl.BlockSpec(memory_space=pltpu.SMEM)] + [hbm] * 4,
        out_specs=(hbm, hbm),
        scratch_shapes=[pltpu.VMEM(operand.shape, f32) for operand in operands]
        + [
            pltpu.VMEM((count, fine + share, width), f32),
            pltpu.VMEM((block_rows, block_cols), b16),
            pltpu.VMEM((block_rows, block_cols), b16),
            pltpu.VMEM((block_cols, block_rows), b16),
            pltpu.VMEM((block_cols, block_rows), b16),
            pltpu.VMEM((count, width, fine + share), b16),
            pltpu.VMEM((count, width, fine + share), b16),
            pltpu.VMEM(win_factor.shape, b16),
            pltpu.VMEM(win_factor.shape, b16),
            pltpu.VMEM(diag_inverse.shape, b16),
            pltpu.VMEM(diag_inverse.shape, b16),
            pltpu.VMEM((count, fine, width), f32),
            pltpu.VMEM((count, fine, width), f32),
            pltpu.VMEM((count, fine, width), f32),
            pltpu.VMEM((ACROSS, n_prow, PIECES, quarter, width), f32),
            pltpu.VMEM((ACROSS, n_pcol, fine, width), f32),
            pltpu.VMEM((ACROSS, 2, n_pcol, fine, width), f32),
            pltpu.VMEM((along, n_pcol, fine, width), f32),
            pltpu.VMEM((along, n_prow, PIECES, quarter, width), f32),
            pltpu.VMEM((along, PIECES, quarter, width), f32),
            pltpu.VMEM((plan.rows, width), f32),
            pltpu.VMEM((plan.rows, width), f32),
            pltpu.VMEM((plan.full, sum(plan.piece), width), f32),
            pltpu.VMEM((plan.full, sum(plan.piece), width), f32),
            dma((len(operands),)),
            dma((2, count)),
            dma((count, PIECES)),
            dma((count,)),
            dma((count, n_prow)),
            dma((count, PIECES)),
            dma((count, n_pcol)),
            dma((count, 2, n_pcol)),
            dma((count, 2, n_pcol)),
            dma((count, 2, n_pcol)),
            dma((count, bits)),
            dma((count, bits)),
            dma((count, PIECES)),
            dma((count,)),
            dma((count, levels)),
            dma((count, levels)),
            dma((count, levels)),
            dma((count, levels)),
        ]
        + [pltpu.VMEM((along, n_prow // 2 ** (bit + 1), PIECES, quarter, width), f32) for bit in range(bits)]
        + [pltpu.VMEM((plan.half_rows[level], width), f32) for level in range(levels)],
        compiler_params=pltpu.CompilerParams(
            collective_id=0, has_side_effects=True, vmem_limit_bytes=48 * 2**20
        ),
    )(readers, *operands)
    anywhere = pl.BlockSpec(memory_space=pl.ANY)
    return pl.pallas_call(
        assemble_kernel,
        out_shape=(
            jax.ShapeDtypeStruct((count, fine, width), f32),
            jax.ShapeDtypeStruct((count, count, width, width), f32),
        ),
        in_specs=[anywhere, anywhere],
        out_specs=(anywhere, anywhere),
        scratch_shapes=[
            pltpu.VMEM((count, fine, width), f32),
            pltpu.VMEM((pairs, width, width), f32),
            pltpu.VMEM((pairs, width, width), f32),
            dma((1 + pairs,)),
            dma((1 + count * count,)),
        ],
        compiler_params=pltpu.CompilerParams(vmem_limit_bytes=16 * 2**20),
    )(panels, blocks)


def per_device(anc_inverse, anc_factor, win_factor, diag_inverse, first_reader):
    n_prow = lax.axis_size("prow")
    n_pcol = lax.axis_size("pcol")
    return sweep(n_prow, n_pcol, first_reader, anc_inverse, anc_factor, win_factor, diag_inverse)


def solution(mesh):
    return jax.shard_map(
        per_device,
        mesh=mesh,
        in_specs=(
            P(("groups", "prow"), "pcol"),
            P("groups", ("prow", "pcol"), None),
            P("groups", None, None),
            P("groups", None, None),
            P("groups"),
        ),
        out_specs=(P("groups", ("prow", "pcol"), None), P("groups", None, None, None)),
        check_vma=False,
    )
```

```python
import functools

import jax
import jax.numpy as jnp
from jax import lax
from jax.experimental import pallas as pl
from jax.experimental.pallas import tpu as pltpu
from jax.sharding import PartitionSpec as P

BLK = 128
PIECES = 4
ORDER = ()
MESH = pl.DeviceIdType.MESH


def split(x):
    high = x.astype(jnp.bfloat16)
    return high, (x - high.astype(jnp.float32)).astype(jnp.bfloat16)


def product(a, b):
    dot = functools.partial(jnp.dot, preferred_element_type=jnp.float32)
    return dot(a[0], b[0]) + (dot(a[0], b[1]) + dot(a[1], b[0]))


def pair_at(first, second):
    return second * (second + 1) // 2 + first


def log2(n):
    return n.bit_length() - 1


class Plan:
    def __init__(self, n_prow, count, width):
        self.bits = log2(n_prow)
        self.blocks = [(first, node) for node in reversed(range(count)) for first in range(node + 1)]
        self.chunks = range(len(self.blocks))
        self.base = [pair_at(*block) * width for block in self.blocks]
        self.width = width
        self.piece = width // n_prow
        self.rows = len(self.blocks) * width

    def half(self, bit):
        return self.width // 2 ** (bit + 1)


def kernel(
    n_prow, n_pcol, plan, readers_ref, a_hbm, f_hbm, win_hbm, diag_hbm, panels_hbm, pairs_hbm,
    a_ref, f_ref, win_ref, diag_ref, v_ref, ath_ref, atl_ref, vh_ref, vl_ref,
    wh_ref, wl_ref, dh_ref, dl_ref, x_ref, s_ref, panel_ref,
    line_ref, turn_ref, y_ref, sum_ref, final_ref, fold_ref, middle_ref,
    load_sem, panel_sem, pairs_sem, line_send, line_recv, relay_send,
    turn_send, turn_recv, y_send, y_recv, w_send, w_recv, back_send, back_recv, z_send, z_recv,
    *more_refs,
):
    loads = [
        pltpu.make_async_copy(source, target, load_sem.at[at])
        for at, (source, target) in enumerate(
            [(f_hbm, f_ref), (a_hbm, a_ref), (diag_hbm, diag_ref), (win_hbm, win_ref)]
        )
    ]
    for load in loads:
        load.start()
    count, fine, width = f_ref.shape
    per_column = n_prow // n_pcol
    quarter = fine // PIECES
    bits = log2(n_prow)
    turn_in = more_refs[:bits]
    half_refs = more_refs[bits:]
    p = lax.axis_index("prow")
    z = lax.axis_index("pcol")
    order = list(reversed(range(count)))
    chunks_of = {node: [c for c in plan.chunks if plan.blocks[c][1] == node] for node in order}

    barrier = pltpu.get_barrier_semaphore()

    def greet(at, carry):
        row, col = at // n_pcol, at % n_pcol

        @pl.when(at != p * n_pcol + z)
        def _():
            pl.semaphore_signal(barrier, inc=1, device_id={"prow": row, "pcol": col}, device_id_type=MESH)

        return carry

    lax.fori_loop(0, n_prow * n_pcol, greet, 0)

    reader = readers_ref[(p * n_pcol + z) * fine // BLK]
    masks = [jnp.where(reader <= node, 1.0, 0.0).astype(jnp.float32) for node in range(count)]

    def rows(start, size):
        return pl.ds(start if isinstance(start, int) else pl.multiple_of(start, 8), size)

    share = v_ref.shape[1] - fine
    unit_row = lax.broadcasted_iota(jnp.int32, (share, width), 0) + (p * n_pcol + z) * share
    unit_col = lax.broadcasted_iota(jnp.int32, (share, width), 1)

    def win_at(first, second):
        at = second * (second - 1) // 2 + first
        return wh_ref[at], wl_ref[at]

    def diag_at(node):
        return dh_ref[node], dl_ref[node]

    def split_factors():
        loads[2].wait()
        loads[3].wait()
        for node in range(count):
            dh_ref[node], dl_ref[node] = split(diag_ref[node])
        for at in range(win_ref.shape[0]):
            wh_ref[at], wl_ref[at] = split(win_ref[at])

    def local_v(node):
        units = jnp.where(unit_row == unit_col + node * width, 1.0, 0.0).astype(jnp.float32)
        total = jnp.concatenate([f_ref[node], units], axis=0)
        for other in range(node + 1, count):
            total = total - product(split(v_ref[other]), win_at(node, other))
        v = product(split(total), diag_at(node))
        v_ref[node] = v
        vh_ref[node], vl_ref[node] = split(v.T)

    def before_x(node):
        total = jnp.zeros((fine, width), jnp.float32)
        for other in range(node + 1, count):
            total = total + product(split(x_ref[other]), win_at(node, other))
        s_ref[node] = total

    def panel_copy(node):
        return pltpu.make_async_copy(panel_ref.at[node], panels_hbm.at[node], panel_sem.at[node])

    def window_part(node, y):
        x = product(split(y - s_ref[node]), diag_at(node))
        x_ref[node] = x
        ends = split(jnp.concatenate([x, v_ref[node, pl.ds(fine, share)]], axis=0))
        for other in range(node + 1):
            sum_ref[pl.ds(pair_at(other, node) * width, width)] = product((vh_ref[other], vl_ref[other]), ends)
        panel_ref[node] = -x * masks[node]
        panel_copy(node).start()

    middle = n_pcol // 2
    lower = z < middle
    beyond = jnp.where(lower, middle, middle - 1)
    toward = jnp.where(lower, z + 1, z - 1)
    outward = jnp.where(lower, z - 1, z + 1)
    depth = jnp.where(lower, z, n_pcol - 1 - z)
    relays = depth == middle - 1

    def line_copy(node, origin, dest, sem):
        return pltpu.make_async_remote_copy(
            src_ref=line_ref.at[node, origin],
            dst_ref=line_ref.at[node, origin],
            send_sem=sem,
            recv_sem=line_recv.at[node, origin],
            device_id={"prow": p, "pcol": dest},
            device_id_type=MESH,
        )

    def same_side(at):
        return lower if at < middle else jnp.logical_not(lower)

    def own_copies(node, run):
        for dest in range(n_pcol):
            @pl.when(jnp.logical_and(z != dest, jnp.logical_or(same_side(dest), beyond == dest)))
            def _():
                run(line_copy(node, z, dest, line_send.at[node, dest]))

    def relay_copies(node, origin, run):
        for dest in range(n_pcol):
            if (origin < middle) != (dest < middle):
                @pl.when(jnp.logical_and(relays, jnp.logical_and(z != dest, same_side(dest))))
                def _():
                    run(line_copy(node, origin, dest, relay_send.at[node, origin, dest]))

    def line_own(node):
        own_copies(node, lambda copy: copy.start())

    def line_wait(node, origin):
        line_copy(node, origin, origin, line_send.at[node, origin]).wait_recv()

    def line_relay(node):
        for origin in range(n_pcol):
            @pl.when(jnp.logical_and(relays, jnp.logical_not(same_side(origin))))
            def _():
                line_wait(node, origin)

            relay_copies(node, origin, lambda copy: copy.start())

    def line_end(node):
        for origin in range(n_pcol):
            here = jnp.logical_or(same_side(origin), jnp.logical_not(relays))

            @pl.when(jnp.logical_and(z != origin, here))
            def _():
                line_wait(node, origin)

    def line_finish(node):
        own_copies(node, lambda copy: copy.wait_send())
        for origin in range(n_pcol):
            relay_copies(node, origin, lambda copy: copy.wait_send())

    def split_turned():
        loads[1].wait()
        turned = split(a_ref[...].T)
        for group in range(n_prow // PIECES):
            for owner in range(PIECES):
                for chunk in range(PIECES):
                    at = (group * PIECES + owner) * fine + chunk * quarter
                    to = (group * PIECES + chunk) * fine + owner * quarter
                    ath_ref[pl.ds(to, quarter)] = turned[0][at : at + quarter]
                    atl_ref[pl.ds(to, quarter)] = turned[1][at : at + quarter]

    turn_starts = [0]
    for bit in range(bits):
        turn_starts.append(turn_starts[bit] + (p // 2**bit) % 2 * (n_prow // 2 ** (bit + 1)))
    slot = turn_starts[bits]

    def mate(axis, bit):
        if axis == "prow":
            return {"prow": p + (1 - (p // 2**bit) % 2 * 2) * 2**bit, "pcol": z}
        return {"prow": p, "pcol": z + (1 - (z // 2**bit) % 2 * 2) * 2**bit}

    def turn_copy(node, bit):
        half = n_prow // 2 ** (bit + 1)
        away = turn_starts[bit] + (1 - (p // 2**bit) % 2) * half
        return pltpu.make_async_remote_copy(
            src_ref=turn_ref.at[node, pl.ds(away, half)],
            dst_ref=turn_in[bit].at[node],
            send_sem=turn_send.at[node, bit],
            recv_sem=turn_recv.at[node, bit],
            device_id=mate("prow", bit),
            device_id_type=MESH,
        )

    def turn_multiply(node):
        gathered = line_ref[node].reshape(a_ref.shape[0], width)
        result = product((ath_ref[...], atl_ref[...]), split(gathered))
        turn_ref[node] = result.reshape(n_prow, PIECES, quarter, width)
        turn_copy(node, 0).start()

    def y_copy(node, owner):
        place = slot // PIECES * PIECES + owner
        return pltpu.make_async_remote_copy(
            src_ref=turn_ref.at[node, slot, owner],
            dst_ref=y_ref.at[node, slot % PIECES],
            send_sem=y_send.at[node, owner],
            recv_sem=y_recv.at[node],
            device_id={"prow": z * per_column + place // n_pcol, "pcol": place % n_pcol},
            device_id_type=MESH,
        )

    def y_mine(owner):
        place = slot // PIECES * PIECES + owner
        return jnp.logical_and(z * per_column + place // n_pcol == p, place % n_pcol == z)

    def turn_step(node, bit):
        turn_copy(node, bit).wait_recv()
        mine = pl.ds(turn_starts[bit + 1], n_prow // 2 ** (bit + 1))
        turn_ref[node, mine] += turn_in[bit][node]
        if bit + 1 < bits:
            turn_copy(node, bit + 1).start()
            return
        for owner in range(PIECES):
            @pl.when(y_mine(owner))
            def _():
                pltpu.make_async_copy(
                    turn_ref.at[node, slot, owner], y_ref.at[node, slot % PIECES], y_recv.at[node]
                ).start()

            @pl.when(jnp.logical_not(y_mine(owner)))
            def _():
                y_copy(node, owner).start()

    def y_end(node):
        pltpu.make_async_copy(y_ref.at[node], y_ref.at[node], y_recv.at[node]).wait()

    def turn_finish(node):
        for bit in range(bits):
            turn_copy(node, bit).wait_send()
        for owner in range(PIECES):
            @pl.when(jnp.logical_not(y_mine(owner)))
            def _():
                y_copy(node, owner).wait_send()

    starts = [0]
    for bit in range(bits):
        starts.append(starts[bit] + (p // 2**bit) % 2 * plan.half(bit))

    def piece_rows(chunk):
        return rows(plan.base[chunk] + starts[bits], plan.piece)

    def chunk_rows(chunk, size):
        return pl.ds(chunk * size, size)

    def w_copy(chunk, bit):
        half = plan.half(bit)
        away = plan.base[chunk] + starts[bit] + (1 - (p // 2**bit) % 2) * half
        return pltpu.make_async_remote_copy(
            src_ref=sum_ref.at[rows(away, half)],
            dst_ref=half_refs[bit].at[chunk_rows(chunk, half)],
            send_sem=w_send.at[chunk, bit],
            recv_sem=w_recv.at[chunk, bit],
            device_id=mate("prow", bit),
            device_id_type=MESH,
        )

    def z_copy(chunk, kind, dest):
        source_ref = final_ref if kind == 2 else sum_ref
        target_ref = (fold_ref, middle_ref)[kind].at[chunk_rows(chunk, plan.piece)] if kind < 2 else None
        return pltpu.make_async_remote_copy(
            src_ref=source_ref.at[piece_rows(chunk)],
            dst_ref=final_ref.at[piece_rows(chunk)] if kind == 2 else target_ref,
            send_sem=z_send.at[chunk, kind],
            recv_sem=z_recv.at[chunk, kind],
            device_id={"prow": p, "pcol": dest},
            device_id_type=MESH,
        )

    def back_copy(chunk, bit):
        part = rows(plan.base[chunk] + starts[bit + 1], plan.half(bit))
        return pltpu.make_async_remote_copy(
            src_ref=final_ref.at[part],
            dst_ref=final_ref.at[part],
            send_sem=back_send.at[chunk, bit],
            recv_sem=back_recv.at[chunk, bit],
            device_id=mate("prow", bit),
            device_id_type=MESH,
        )

    def pairs_copy(chunk):
        part = pl.ds(plan.base[chunk], width)
        return pltpu.make_async_copy(final_ref.at[part], pairs_hbm.at[part], pairs_sem.at[chunk])

    def inward(chunk):
        @pl.when(depth < middle - 1)
        def _():
            z_copy(chunk, 0, toward).start()

        @pl.when(relays)
        def _():
            z_copy(chunk, 1, toward).start()

    def w_step(chunk, bit):
        w_copy(chunk, bit).wait_recv()
        half = plan.half(bit)
        mine = rows(plan.base[chunk] + starts[bit + 1], half)
        sum_ref[mine] += half_refs[bit][chunk_rows(chunk, half)]
        if bit + 1 < bits:
            w_copy(chunk, bit + 1).start()
        else:
            @pl.when(depth == 0)
            def _():
                inward(chunk)

    def fold_step(chunk, step):
        @pl.when(depth == step)
        def _():
            z_copy(chunk, 0, outward).wait_recv()
            sum_ref[piece_rows(chunk)] += fold_ref[chunk_rows(chunk, plan.piece)]
            inward(chunk)

    def outgoing(chunk):
        @pl.when(depth > 0)
        def _():
            z_copy(chunk, 2, outward).start()

        back_copy(chunk, bits - 1).start()

    def middle_step(chunk):
        @pl.when(relays)
        def _():
            z_copy(chunk, 1, toward).wait_recv()
            final_ref[piece_rows(chunk)] = sum_ref[piece_rows(chunk)] + middle_ref[chunk_rows(chunk, plan.piece)]
            outgoing(chunk)

    def unfold_step(chunk, step):
        @pl.when(depth == step)
        def _():
            z_copy(chunk, 2, toward).wait_recv()
            outgoing(chunk)

    def back_step(chunk, bit):
        back_copy(chunk, bit).wait_recv()
        if bit > 0:
            back_copy(chunk, bit - 1).start()
        else:
            pairs_copy(chunk).start()

    def window_finish(chunk):
        for bit in range(bits):
            w_copy(chunk, bit).wait_send()
            back_copy(chunk, bit).wait_send()

        @pl.when(depth < middle - 1)
        def _():
            z_copy(chunk, 0, toward).wait_send()

        @pl.when(relays)
        def _():
            z_copy(chunk, 1, toward).wait_send()

        @pl.when(depth > 0)
        def _():
            z_copy(chunk, 2, outward).wait_send()

        pairs_copy(chunk).wait()

    def close(node):
        window_part(node, y_ref[node].reshape(fine, width))
        for chunk in chunks_of[node]:
            w_copy(chunk, 0).start()

    stages, due = {}, {}

    def at(time, name, run, *args):
        stages[name] = functools.partial(run, *args)
        due[name] = (time, len(due))

    at(0.0, ("bar",), pl.semaphore_wait, barrier, n_prow * n_pcol - 1)
    latest = 0.0
    for turn, node in enumerate(order):
        at(5.0 + turn, ("v", node), local_v, node)
        start = 8.0 * turn
        at(max(0.1, start - 2.0), ("l", node, 0), line_own, node)
        at(start + 8.0, ("l", node, 1), line_relay, node)
        at(start + 14.0, ("l", node, 3), line_end, node)
        done = start + 14.1
        at(done, ("tm", node), turn_multiply, node)
        for bit in range(bits):
            done += 2.0 if bit == 0 else 5.0
            at(done, ("t", node, bit), turn_step, node, bit)
        latest = max(done + 5.0, latest + 2.0)
        at(latest - 1.0, ("b", node), before_x, node)
        at(latest, ("y", node), y_end, node)
        at(latest, ("x", node), close, node)
        for turn_w, chunk in enumerate(chunks_of[node]):
            time = latest + 2.0 * turn_w
            for bit in range(bits):
                time += 2.0 if bit == 0 else 4.0
                at(time, ("w", chunk, bit), w_step, chunk, bit)
            for step in range(1, middle):
                time += 4.0
                at(time, ("w", chunk, bits + step - 1), fold_step, chunk, step)
            time += 4.0
            at(time, ("w", chunk, bits + middle - 1), middle_step, chunk)
            for step in reversed(range(middle - 1)):
                time += 4.0
                at(time, ("k", chunk, bits + step), unfold_step, chunk, step)
            for bit in reversed(range(bits)):
                time += 4.0 if bit else 2.0
                at(time, ("k", chunk, bit), back_step, chunk, bit)

    sequence = ORDER if set(ORDER) == set(stages) else sorted(stages, key=due.get)
    loads[0].wait()
    for node in range(count):
        f_ref[node] = f_ref[node] * masks[node]
        line_ref[node, z] = f_ref[node]
    split_turned()
    split_factors()
    for name in sequence:
        stages[name]()
    for node in order:
        line_finish(node)
        turn_finish(node)
        panel_copy(node).wait()
    for chunk in plan.chunks:
        window_finish(chunk)


def assemble_kernel(panels_in, pairs_in, panels_out, window_out, panel_ref, pairs_ref, turned_ref, in_sem, out_sem):
    count, _, width = panels_in.shape
    into = pltpu.make_async_copy(panels_in, panel_ref, in_sem.at[0])
    into.start()
    order = [(first, second) for second in reversed(range(count)) for first in range(second + 1)]

    def load(first, second):
        at = pair_at(first, second)
        return pltpu.make_async_copy(pairs_in.at[pl.ds(at * width, width)], pairs_ref.at[at], in_sem.at[1 + at])

    for first, second in order:
        load(first, second).start()
    stores = []
    for first, second in order:
        at = pair_at(first, second)
        load(first, second).wait()
        stores.append(pltpu.make_async_copy(pairs_ref.at[at], window_out.at[first, second], out_sem.at[1 + len(stores)]))
        stores[-1].start()
        if first != second:
            turned_ref[at] = pairs_ref[at].T
            stores.append(
                pltpu.make_async_copy(turned_ref.at[at], window_out.at[second, first], out_sem.at[1 + len(stores)])
            )
            stores[-1].start()
    into.wait()
    stores.append(pltpu.make_async_copy(panel_ref, panels_out, out_sem.at[0]))
    stores[-1].start()
    for store in stores:
        store.wait()


def sweep(n_prow, n_pcol, readers, anc_inverse, anc_factor, win_factor, diag_inverse):
    count, fine, width = anc_factor.shape
    pairs = count * (count + 1) // 2
    share = count * width // (n_prow * n_pcol)
    bits = log2(n_prow)
    quarter = fine // PIECES
    plan = Plan(n_prow, count, width)
    chunks = len(plan.chunks)
    block_rows, block_cols = anc_inverse.shape
    hbm = pl.BlockSpec(memory_space=pltpu.HBM)
    operands = (anc_inverse, anc_factor, win_factor, diag_inverse)
    f32, b16 = jnp.float32, jnp.bfloat16
    dma = pltpu.SemaphoreType.DMA
    panels, blocks = pl.pallas_call(
        functools.partial(kernel, n_prow, n_pcol, plan),
        out_shape=(
            jax.ShapeDtypeStruct((count, fine, width), f32),
            jax.ShapeDtypeStruct((pairs * width, width), f32),
        ),
        in_specs=[pl.BlockSpec(memory_space=pltpu.SMEM)] + [hbm] * 4,
        out_specs=(hbm, hbm),
        scratch_shapes=[pltpu.VMEM(operand.shape, f32) for operand in operands]
        + [
            pltpu.VMEM((count, fine + share, width), f32),
            pltpu.VMEM((block_cols, block_rows), b16),
            pltpu.VMEM((block_cols, block_rows), b16),
            pltpu.VMEM((count, width, fine + share), b16),
            pltpu.VMEM((count, width, fine + share), b16),
            pltpu.VMEM(win_factor.shape, b16),
            pltpu.VMEM(win_factor.shape, b16),
            pltpu.VMEM(diag_inverse.shape, b16),
            pltpu.VMEM(diag_inverse.shape, b16),
            pltpu.VMEM((count, fine, width), f32),
            pltpu.VMEM((count, fine, width), f32),
            pltpu.VMEM((count, fine, width), f32),
            pltpu.VMEM((count, n_pcol, fine, width), f32),
            pltpu.VMEM((count, n_prow, PIECES, quarter, width), f32),
            pltpu.VMEM((count, PIECES, quarter, width), f32),
            pltpu.VMEM((plan.rows, width), f32),
            pltpu.VMEM((plan.rows, width), f32),
            pltpu.VMEM((chunks * plan.piece, width), f32),
            pltpu.VMEM((chunks * plan.piece, width), f32),
            dma((len(operands),)),
            dma((count,)),
            dma((chunks,)),
            dma((count, n_pcol)),
            dma((count, n_pcol)),
            dma((count, n_pcol, n_pcol)),
            dma((count, bits)),
            dma((count, bits)),
            dma((count, PIECES)),
            dma((count,)),
            dma((chunks, bits)),
            dma((chunks, bits)),
            dma((chunks, bits)),
            dma((chunks, bits)),
            dma((chunks, 3)),
            dma((chunks, 3)),
        ]
        + [pltpu.VMEM((count, n_prow // 2 ** (bit + 1), PIECES, quarter, width), f32) for bit in range(bits)]
        + [pltpu.VMEM((chunks * plan.half(bit), width), f32) for bit in range(bits)],
        compiler_params=pltpu.CompilerParams(
            collective_id=0, has_side_effects=True, vmem_limit_bytes=58 * 2**20
        ),
    )(readers, *operands)
    return pl.pallas_call(
        assemble_kernel,
        out_shape=(
            jax.ShapeDtypeStruct((count, fine, width), f32),
            jax.ShapeDtypeStruct((count, count, width, width), f32),
        ),
        in_specs=[hbm, hbm],
        out_specs=(hbm, hbm),
        scratch_shapes=[
            pltpu.VMEM((count, fine, width), f32),
            pltpu.VMEM((pairs, width, width), f32),
            pltpu.VMEM((pairs, width, width), f32),
            dma((1 + pairs,)),
            dma((1 + count * count,)),
        ],
        compiler_params=pltpu.CompilerParams(vmem_limit_bytes=60 * 2**20),
    )(panels, blocks)


def per_device(anc_inverse, anc_factor, win_factor, diag_inverse, first_reader):
    n_prow = lax.axis_size("prow")
    n_pcol = lax.axis_size("pcol")
    return sweep(n_prow, n_pcol, first_reader, anc_inverse, anc_factor, win_factor, diag_inverse)


def solution(mesh):
    return jax.shard_map(
        per_device,
        mesh=mesh,
        in_specs=(
            P(("groups", "prow"), "pcol"),
            P("groups", ("prow", "pcol"), None),
            P("groups", None, None),
            P("groups", None, None),
            P("groups"),
        ),
        out_specs=(P("groups", ("prow", "pcol"), None), P("groups", None, None, None)),
        check_vma=False,
    )
```

```python
import functools

import jax
import jax.numpy as jnp
from jax import lax
from jax.experimental import pallas as pl
from jax.experimental.pallas import tpu as pltpu
from jax.sharding import PartitionSpec as P

BLK = 128
PIECES = 4
DIRECT = (0,)
ORDER = ()
MESH = pl.DeviceIdType.MESH


def split(x):
    high = x.astype(jnp.bfloat16)
    return high, (x - high.astype(jnp.float32)).astype(jnp.bfloat16)


def product(a, b):
    dot = functools.partial(jnp.dot, preferred_element_type=jnp.float32)
    return dot(a[0], b[0]) + (dot(a[0], b[1]) + dot(a[1], b[0]))


def pair_at(first, second):
    return second * (second + 1) // 2 + first


def log2(n):
    return n.bit_length() - 1


class Plan:
    def __init__(self, n_prow, count, width):
        self.bits = log2(n_prow)
        self.blocks = [(first, node) for node in reversed(range(count)) for first in range(node + 1)]
        self.chunks = range(len(self.blocks))
        self.base = [pair_at(*block) * width for block in self.blocks]
        self.width = width
        self.piece = width // n_prow
        self.rows = len(self.blocks) * width

    def half(self, bit):
        return self.width // 2 ** (bit + 1)


def kernel(
    n_prow, n_pcol, plan, readers_ref, a_hbm, f_hbm, win_hbm, diag_hbm, panels_hbm, pairs_hbm,
    a_ref, f_ref, win_ref, diag_ref, v_ref, ath_ref, atl_ref, vh_ref, vl_ref,
    wh_ref, wl_ref, dh_ref, dl_ref, x_ref, s_ref, panel_ref,
    line_ref, turn_ref, y_ref, sum_ref, final_ref, fold_ref, middle_ref, direct_ref,
    load_sem, panel_sem, pairs_sem, line_send, line_recv,
    turn_send, turn_recv, y_send, y_recv, w_send, w_recv, back_send, back_recv, z_send, z_recv, direct_send, direct_recv,
    *more_refs,
):
    loads = [
        pltpu.make_async_copy(source, target, load_sem.at[at])
        for at, (source, target) in enumerate(
            [(f_hbm, f_ref), (a_hbm, a_ref), (diag_hbm, diag_ref), (win_hbm, win_ref)]
        )
    ]
    for load in loads:
        load.start()
    count, fine, width = f_ref.shape
    per_column = n_prow // n_pcol
    quarter = fine // PIECES
    bits = log2(n_prow)
    turn_in = more_refs[:bits]
    half_refs = more_refs[bits:]
    p = lax.axis_index("prow")
    z = lax.axis_index("pcol")
    order = list(reversed(range(count)))
    chunks_of = {node: [c for c in plan.chunks if plan.blocks[c][1] == node] for node in order}

    barrier = pltpu.get_barrier_semaphore()

    def greet(dest):
        pl.semaphore_signal(barrier, inc=1, device_id=dest, device_id_type=MESH)

    @pl.when(z > 0)
    def _():
        greet({"prow": p, "pcol": z - 1})

    @pl.when(z < n_pcol - 1)
    def _():
        greet({"prow": p, "pcol": z + 1})

    for bit in range(bits):
        greet({"prow": p + (1 - (p // 2**bit) % 2 * 2) * 2**bit, "pcol": z})
    greeted = bits + jnp.where(z > 0, 1, 0) + jnp.where(z < n_pcol - 1, 1, 0)

    reader = readers_ref[(p * n_pcol + z) * fine // BLK]
    masks = [jnp.where(reader <= node, 1.0, 0.0).astype(jnp.float32) for node in range(count)]

    def rows(start, size):
        return pl.ds(start if isinstance(start, int) else pl.multiple_of(start, 8), size)

    share = v_ref.shape[1] - fine
    unit_row = lax.broadcasted_iota(jnp.int32, (share, width), 0) + (p * n_pcol + z) * share
    unit_col = lax.broadcasted_iota(jnp.int32, (share, width), 1)

    def win_at(first, second):
        at = second * (second - 1) // 2 + first
        return wh_ref[at], wl_ref[at]

    def diag_at(node):
        return dh_ref[node], dl_ref[node]

    def split_factors():
        loads[2].wait()
        loads[3].wait()
        for node in range(count):
            dh_ref[node], dl_ref[node] = split(diag_ref[node])
        for at in range(win_ref.shape[0]):
            wh_ref[at], wl_ref[at] = split(win_ref[at])

    def local_v(node):
        units = jnp.where(unit_row == unit_col + node * width, 1.0, 0.0).astype(jnp.float32)
        total = jnp.concatenate([f_ref[node], units], axis=0)
        for other in range(node + 1, count):
            total = total - product(split(v_ref[other]), win_at(node, other))
        v = product(split(total), diag_at(node))
        v_ref[node] = v
        vh_ref[node], vl_ref[node] = split(v.T)

    def before_x(node):
        total = jnp.zeros((fine, width), jnp.float32)
        for other in range(node + 1, count):
            total = total + product(split(x_ref[other]), win_at(node, other))
        s_ref[node] = total

    def panel_copy(node):
        return pltpu.make_async_copy(panel_ref.at[node], panels_hbm.at[node], panel_sem.at[node])

    def window_part(node, y):
        x = product(split(y - s_ref[node]), diag_at(node))
        x_ref[node] = x
        ends = split(jnp.concatenate([x, v_ref[node, pl.ds(fine, share)]], axis=0))
        for other in range(node + 1):
            sum_ref[pl.ds(pair_at(other, node) * width, width)] = product((vh_ref[other], vl_ref[other]), ends)
        panel_ref[node] = -x * masks[node]
        panel_copy(node).start()

    middle = n_pcol // 2
    lower = z < middle
    beyond = jnp.where(lower, middle, middle - 1)
    toward = jnp.where(lower, z + 1, z - 1)
    outward = jnp.where(lower, z - 1, z + 1)
    depth = jnp.where(lower, z, n_pcol - 1 - z)
    relays = depth == middle - 1

    def line_copy(node, origin, dest, sem):
        return pltpu.make_async_remote_copy(
            src_ref=line_ref.at[node, origin],
            dst_ref=line_ref.at[node, origin],
            send_sem=sem,
            recv_sem=line_recv.at[node, origin],
            device_id={"prow": p, "pcol": dest},
            device_id_type=MESH,
        )

    def line_side(side, back):
        return z - back if side == 0 else z + back

    def line_sends(side, hop):
        if side == 0:
            return jnp.logical_and(z >= hop, z < n_pcol - 1)
        return jnp.logical_and(z + hop < n_pcol, z > 0)

    def line_gets(side, hop):
        return z - 1 - hop >= 0 if side == 0 else z + 1 + hop < n_pcol

    def line_step(node, hop):
        for side in (0, 1):
            if hop > 0:
                @pl.when(line_gets(side, hop - 1))
                def _():
                    line_copy(node, line_side(side, hop), line_side(side, 1), line_send.at[node, side, hop - 1]).wait_recv()

            if hop < n_pcol - 1:
                @pl.when(line_sends(side, hop))
                def _():
                    line_copy(node, line_side(side, hop), line_side(side, -1), line_send.at[node, side, hop]).start()

    def line_finish(node):
        for hop in range(n_pcol - 1):
            for side in (0, 1):
                @pl.when(line_sends(side, hop))
                def _():
                    line_copy(node, line_side(side, hop), line_side(side, -1), line_send.at[node, side, hop]).wait_send()

    def split_turned():
        loads[1].wait()
        turned = split(a_ref[...].T)
        for group in range(n_prow // PIECES):
            for owner in range(PIECES):
                for chunk in range(PIECES):
                    at = (group * PIECES + owner) * fine + chunk * quarter
                    to = (group * PIECES + chunk) * fine + owner * quarter
                    ath_ref[pl.ds(to, quarter)] = turned[0][at : at + quarter]
                    atl_ref[pl.ds(to, quarter)] = turned[1][at : at + quarter]

    turn_starts = [0]
    for bit in range(bits):
        turn_starts.append(turn_starts[bit] + (p // 2**bit) % 2 * (n_prow // 2 ** (bit + 1)))
    slot = turn_starts[bits]

    def mate(axis, bit):
        if axis == "prow":
            return {"prow": p + (1 - (p // 2**bit) % 2 * 2) * 2**bit, "pcol": z}
        return {"prow": p, "pcol": z + (1 - (z // 2**bit) % 2 * 2) * 2**bit}

    def turn_copy(node, bit):
        half = n_prow // 2 ** (bit + 1)
        away = turn_starts[bit] + (1 - (p // 2**bit) % 2) * half
        return pltpu.make_async_remote_copy(
            src_ref=turn_ref.at[node, pl.ds(away, half)],
            dst_ref=turn_in[bit].at[node],
            send_sem=turn_send.at[node, bit],
            recv_sem=turn_recv.at[node, bit],
            device_id=mate("prow", bit),
            device_id_type=MESH,
        )

    def turn_multiply(node):
        gathered = line_ref[node].reshape(a_ref.shape[0], width)
        result = product((ath_ref[...], atl_ref[...]), split(gathered))
        turn_ref[node] = result.reshape(n_prow, PIECES, quarter, width)
        turn_copy(node, 0).start()

    def y_copy(node, owner):
        place = slot // PIECES * PIECES + owner
        return pltpu.make_async_remote_copy(
            src_ref=turn_ref.at[node, slot, owner],
            dst_ref=y_ref.at[node, slot % PIECES],
            send_sem=y_send.at[node, owner],
            recv_sem=y_recv.at[node],
            device_id={"prow": z * per_column + place // n_pcol, "pcol": place % n_pcol},
            device_id_type=MESH,
        )

    def y_mine(owner):
        place = slot // PIECES * PIECES + owner
        return jnp.logical_and(z * per_column + place // n_pcol == p, place % n_pcol == z)

    def turn_step(node, bit):
        turn_copy(node, bit).wait_recv()
        mine = pl.ds(turn_starts[bit + 1], n_prow // 2 ** (bit + 1))
        turn_ref[node, mine] += turn_in[bit][node]
        if bit + 1 < bits:
            turn_copy(node, bit + 1).start()
            return
        for owner in range(PIECES):
            @pl.when(y_mine(owner))
            def _():
                pltpu.make_async_copy(
                    turn_ref.at[node, slot, owner], y_ref.at[node, slot % PIECES], y_recv.at[node]
                ).start()

            @pl.when(jnp.logical_not(y_mine(owner)))
            def _():
                y_copy(node, owner).start()

    def y_end(node):
        pltpu.make_async_copy(y_ref.at[node], y_ref.at[node], y_recv.at[node]).wait()

    def turn_finish(node):
        for bit in range(bits):
            turn_copy(node, bit).wait_send()
        for owner in range(PIECES):
            @pl.when(jnp.logical_not(y_mine(owner)))
            def _():
                y_copy(node, owner).wait_send()

    starts = [0]
    for bit in range(bits):
        starts.append(starts[bit] + (p // 2**bit) % 2 * plan.half(bit))

    def piece_rows(chunk):
        return rows(plan.base[chunk] + starts[bits], plan.piece)

    def chunk_rows(chunk, size):
        return pl.ds(chunk * size, size)

    def w_copy(chunk, bit):
        half = plan.half(bit)
        away = plan.base[chunk] + starts[bit] + (1 - (p // 2**bit) % 2) * half
        return pltpu.make_async_remote_copy(
            src_ref=sum_ref.at[rows(away, half)],
            dst_ref=half_refs[bit].at[chunk_rows(chunk, half)],
            send_sem=w_send.at[chunk, bit],
            recv_sem=w_recv.at[chunk, bit],
            device_id=mate("prow", bit),
            device_id_type=MESH,
        )

    def z_copy(chunk, kind, dest):
        source_ref = final_ref if kind == 2 else sum_ref
        target_ref = (fold_ref, middle_ref)[kind].at[chunk_rows(chunk, plan.piece)] if kind < 2 else None
        return pltpu.make_async_remote_copy(
            src_ref=source_ref.at[piece_rows(chunk)],
            dst_ref=final_ref.at[piece_rows(chunk)] if kind == 2 else target_ref,
            send_sem=z_send.at[chunk, kind],
            recv_sem=z_recv.at[chunk, kind],
            device_id={"prow": p, "pcol": dest},
            device_id_type=MESH,
        )

    def back_copy(chunk, bit):
        part = rows(plan.base[chunk] + starts[bit + 1], plan.half(bit))
        return pltpu.make_async_remote_copy(
            src_ref=final_ref.at[part],
            dst_ref=final_ref.at[part],
            send_sem=back_send.at[chunk, bit],
            recv_sem=back_recv.at[chunk, bit],
            device_id=mate("prow", bit),
            device_id_type=MESH,
        )

    def pairs_copy(chunk):
        part = pl.ds(plan.base[chunk], width)
        return pltpu.make_async_copy(final_ref.at[part], pairs_hbm.at[part], pairs_sem.at[chunk])

    members = n_prow // 2 * n_pcol
    member = p // 2 * n_pcol + z
    small = plan.half(0) // members
    direct = [c for c in plan.chunks if plan.blocks[c][1] in DIRECT and small % 8 == 0]

    def member_rows(chunk, at):
        return rows(plan.base[chunk] + starts[1] + at * small, small)

    def member_copy(chunk, kind, sender, dest):
        place = direct.index(chunk)
        if kind == 0:
            source_ref, target_ref = sum_ref.at[member_rows(chunk, dest)], direct_ref.at[place, sender]
        else:
            source_ref = target_ref = final_ref.at[member_rows(chunk, sender)]
        return pltpu.make_async_remote_copy(
            src_ref=source_ref,
            dst_ref=target_ref,
            send_sem=direct_send.at[place, kind, dest],
            recv_sem=direct_recv.at[place, kind, sender],
            device_id={"prow": dest // n_pcol * 2 + p % 2, "pcol": dest % n_pcol},
            device_id_type=MESH,
        )

    def members_but(run):
        for at in range(members):
            @pl.when(member != at)
            def _():
                run(at)

    def direct_start(chunk):
        w_copy(chunk, 0).wait_recv()
        half = plan.half(0)
        mine = rows(plan.base[chunk] + starts[1], half)
        sum_ref[mine] += half_refs[0][chunk_rows(chunk, half)]
        members_but(lambda at: member_copy(chunk, 0, member, at).start())

    def direct_sum(chunk):
        place = direct.index(chunk)
        direct_ref[place, member] = sum_ref[member_rows(chunk, member)]
        members_but(lambda at: member_copy(chunk, 0, at, at).wait_recv())
        total = direct_ref[place, 0]
        for at in range(1, members):
            total = total + direct_ref[place, at]
        final_ref[member_rows(chunk, member)] = total
        members_but(lambda at: member_copy(chunk, 1, member, at).start())

    def direct_end(chunk):
        members_but(lambda at: member_copy(chunk, 1, at, at).wait_recv())
        back_copy(chunk, 0).start()

    def direct_finish(chunk):
        w_copy(chunk, 0).wait_send()
        back_copy(chunk, 0).wait_send()
        for kind in (0, 1):
            members_but(lambda at: member_copy(chunk, kind, member, at).wait_send())
        pairs_copy(chunk).wait()

    def inward(chunk):
        @pl.when(depth < middle - 1)
        def _():
            z_copy(chunk, 0, toward).start()

        @pl.when(relays)
        def _():
            z_copy(chunk, 1, toward).start()

    def w_step(chunk, bit):
        w_copy(chunk, bit).wait_recv()
        half = plan.half(bit)
        mine = rows(plan.base[chunk] + starts[bit + 1], half)
        sum_ref[mine] += half_refs[bit][chunk_rows(chunk, half)]
        if bit + 1 < bits:
            w_copy(chunk, bit + 1).start()
        else:
            @pl.when(depth == 0)
            def _():
                inward(chunk)

    def fold_step(chunk, step):
        @pl.when(depth == step)
        def _():
            z_copy(chunk, 0, outward).wait_recv()
            sum_ref[piece_rows(chunk)] += fold_ref[chunk_rows(chunk, plan.piece)]
            inward(chunk)

    def outgoing(chunk):
        @pl.when(depth > 0)
        def _():
            z_copy(chunk, 2, outward).start()

        back_copy(chunk, bits - 1).start()

    def middle_step(chunk):
        @pl.when(relays)
        def _():
            z_copy(chunk, 1, toward).wait_recv()
            final_ref[piece_rows(chunk)] = sum_ref[piece_rows(chunk)] + middle_ref[chunk_rows(chunk, plan.piece)]
            outgoing(chunk)

    def unfold_step(chunk, step):
        @pl.when(depth == step)
        def _():
            z_copy(chunk, 2, toward).wait_recv()
            outgoing(chunk)

    def back_step(chunk, bit):
        back_copy(chunk, bit).wait_recv()
        if bit > 0:
            back_copy(chunk, bit - 1).start()
        else:
            pairs_copy(chunk).start()

    def window_finish(chunk):
        for bit in range(bits):
            w_copy(chunk, bit).wait_send()
            back_copy(chunk, bit).wait_send()

        @pl.when(depth < middle - 1)
        def _():
            z_copy(chunk, 0, toward).wait_send()

        @pl.when(relays)
        def _():
            z_copy(chunk, 1, toward).wait_send()

        @pl.when(depth > 0)
        def _():
            z_copy(chunk, 2, outward).wait_send()

        pairs_copy(chunk).wait()

    def close(node):
        window_part(node, y_ref[node].reshape(fine, width))
        for chunk in chunks_of[node]:
            w_copy(chunk, 0).start()

    stages, due = {}, {}

    def at(time, name, run, *args):
        stages[name] = functools.partial(run, *args)
        due[name] = (time, len(due))

    at(0.0, ("bar",), pl.semaphore_wait, barrier, greeted)
    latest = 0.0
    for turn, node in enumerate(order):
        at(5.0 + turn, ("v", node), local_v, node)
        start = 8.0 * turn
        hops = n_pcol - 1
        at(0.1 + start, ("l", node, 0), line_step, node, 0)
        for hop in range(1, hops + 1):
            at(0.1 + start + 5.0 * hop, ("l", node, hop), line_step, node, hop)
        done = 0.2 + start + 5.0 * hops
        at(done, ("tm", node), turn_multiply, node)
        for bit in range(bits):
            done += 2.0 if bit == 0 else 5.0
            at(done, ("t", node, bit), turn_step, node, bit)
        latest = max(done + 5.0, latest + 2.0)
        at(latest - 1.0, ("b", node), before_x, node)
        at(latest, ("y", node), y_end, node)
        at(latest, ("x", node), close, node)
        for turn_w, chunk in enumerate(chunks_of[node]):
            time = latest + 2.0 * turn_w
            if chunk in direct:
                at(time + 2.0, ("w", chunk, 0), direct_start, chunk)
                at(time + 8.0, ("d", chunk, 0), direct_sum, chunk)
                at(time + 14.0, ("d", chunk, 1), direct_end, chunk)
                at(time + 16.0, ("k", chunk, 0), back_step, chunk, 0)
                continue
            for bit in range(bits):
                time += 2.0 if bit == 0 else 4.0
                at(time, ("w", chunk, bit), w_step, chunk, bit)
            for step in range(1, middle):
                time += 4.0
                at(time, ("w", chunk, bits + step - 1), fold_step, chunk, step)
            time += 4.0
            at(time, ("w", chunk, bits + middle - 1), middle_step, chunk)
            for step in reversed(range(middle - 1)):
                time += 4.0
                at(time, ("k", chunk, bits + step), unfold_step, chunk, step)
            for bit in reversed(range(bits)):
                time += 4.0 if bit else 2.0
                at(time, ("k", chunk, bit), back_step, chunk, bit)

    sequence = ORDER if set(ORDER) == set(stages) else sorted(stages, key=due.get)
    loads[0].wait()
    for node in range(count):
        f_ref[node] = f_ref[node] * masks[node]
        line_ref[node, z] = f_ref[node]
    split_turned()
    split_factors()
    for name in sequence:
        stages[name]()
    for node in order:
        line_finish(node)
        turn_finish(node)
        panel_copy(node).wait()
    for chunk in plan.chunks:
        (direct_finish if chunk in direct else window_finish)(chunk)


def assemble_kernel(panels_in, pairs_in, panels_out, window_out, panel_ref, pairs_ref, turned_ref, in_sem, out_sem):
    count, _, width = panels_in.shape
    into = pltpu.make_async_copy(panels_in, panel_ref, in_sem.at[0])
    into.start()
    order = [(first, second) for second in reversed(range(count)) for first in range(second + 1)]

    def load(first, second):
        at = pair_at(first, second)
        return pltpu.make_async_copy(pairs_in.at[pl.ds(at * width, width)], pairs_ref.at[at], in_sem.at[1 + at])

    for first, second in order:
        load(first, second).start()
    stores = []
    for first, second in order:
        at = pair_at(first, second)
        load(first, second).wait()
        stores.append(pltpu.make_async_copy(pairs_ref.at[at], window_out.at[first, second], out_sem.at[1 + len(stores)]))
        stores[-1].start()
        if first != second:
            turned_ref[at] = pairs_ref[at].T
            stores.append(
                pltpu.make_async_copy(turned_ref.at[at], window_out.at[second, first], out_sem.at[1 + len(stores)])
            )
            stores[-1].start()
    into.wait()
    stores.append(pltpu.make_async_copy(panel_ref, panels_out, out_sem.at[0]))
    stores[-1].start()
    for store in stores:
        store.wait()


def sweep(n_prow, n_pcol, readers, anc_inverse, anc_factor, win_factor, diag_inverse):
    count, fine, width = anc_factor.shape
    pairs = count * (count + 1) // 2
    share = count * width // (n_prow * n_pcol)
    bits = log2(n_prow)
    quarter = fine // PIECES
    plan = Plan(n_prow, count, width)
    chunks = len(plan.chunks)
    members = n_prow // 2 * n_pcol
    block_rows, block_cols = anc_inverse.shape
    hbm = pl.BlockSpec(memory_space=pltpu.HBM)
    operands = (anc_inverse, anc_factor, win_factor, diag_inverse)
    f32, b16 = jnp.float32, jnp.bfloat16
    dma = pltpu.SemaphoreType.DMA
    panels, blocks = pl.pallas_call(
        functools.partial(kernel, n_prow, n_pcol, plan),
        out_shape=(
            jax.ShapeDtypeStruct((count, fine, width), f32),
            jax.ShapeDtypeStruct((pairs * width, width), f32),
        ),
        in_specs=[pl.BlockSpec(memory_space=pltpu.SMEM)] + [hbm] * 4,
        out_specs=(hbm, hbm),
        scratch_shapes=[pltpu.VMEM(operand.shape, f32) for operand in operands]
        + [
            pltpu.VMEM((count, fine + share, width), f32),
            pltpu.VMEM((block_cols, block_rows), b16),
            pltpu.VMEM((block_cols, block_rows), b16),
            pltpu.VMEM((count, width, fine + share), b16),
            pltpu.VMEM((count, width, fine + share), b16),
            pltpu.VMEM(win_factor.shape, b16),
            pltpu.VMEM(win_factor.shape, b16),
            pltpu.VMEM(diag_inverse.shape, b16),
            pltpu.VMEM(diag_inverse.shape, b16),
            pltpu.VMEM((count, fine, width), f32),
            pltpu.VMEM((count, fine, width), f32),
            pltpu.VMEM((count, fine, width), f32),
            pltpu.VMEM((count, n_pcol, fine, width), f32),
            pltpu.VMEM((count, n_prow, PIECES, quarter, width), f32),
            pltpu.VMEM((count, PIECES, quarter, width), f32),
            pltpu.VMEM((plan.rows, width), f32),
            pltpu.VMEM((plan.rows, width), f32),
            pltpu.VMEM((chunks * plan.piece, width), f32),
            pltpu.VMEM((chunks * plan.piece, width), f32),
            pltpu.VMEM((sum(DIRECT) + len(DIRECT), members, max(8, width // 2 // members), width), f32),
            dma((len(operands),)),
            dma((count,)),
            dma((chunks,)),
            dma((count, 2, n_pcol)),
            dma((count, n_pcol)),
            dma((count, bits)),
            dma((count, bits)),
            dma((count, PIECES)),
            dma((count,)),
            dma((chunks, bits)),
            dma((chunks, bits)),
            dma((chunks, bits)),
            dma((chunks, bits)),
            dma((chunks, 3)),
            dma((chunks, 3)),
            dma((sum(DIRECT) + len(DIRECT), 2, members)),
            dma((sum(DIRECT) + len(DIRECT), 2, members)),
        ]
        + [pltpu.VMEM((count, n_prow // 2 ** (bit + 1), PIECES, quarter, width), f32) for bit in range(bits)]
        + [pltpu.VMEM((chunks * plan.half(bit), width), f32) for bit in range(bits)],
        compiler_params=pltpu.CompilerParams(
            collective_id=0, has_side_effects=True, vmem_limit_bytes=58 * 2**20
        ),
    )(readers, *operands)
    return pl.pallas_call(
        assemble_kernel,
        out_shape=(
            jax.ShapeDtypeStruct((count, fine, width), f32),
            jax.ShapeDtypeStruct((count, count, width, width), f32),
        ),
        in_specs=[hbm, hbm],
        out_specs=(hbm, hbm),
        scratch_shapes=[
            pltpu.VMEM((count, fine, width), f32),
            pltpu.VMEM((pairs, width, width), f32),
            pltpu.VMEM((pairs, width, width), f32),
            dma((1 + pairs,)),
            dma((1 + count * count,)),
        ],
        compiler_params=pltpu.CompilerParams(vmem_limit_bytes=60 * 2**20),
    )(panels, blocks)


def per_device(anc_inverse, anc_factor, win_factor, diag_inverse, first_reader):
    n_prow = lax.axis_size("prow")
    n_pcol = lax.axis_size("pcol")
    return sweep(n_prow, n_pcol, first_reader, anc_inverse, anc_factor, win_factor, diag_inverse)


def solution(mesh):
    return jax.shard_map(
        per_device,
        mesh=mesh,
        in_specs=(
            P(("groups", "prow"), "pcol"),
            P("groups", ("prow", "pcol"), None),
            P("groups", None, None),
            P("groups", None, None),
            P("groups"),
        ),
        out_specs=(P("groups", ("prow", "pcol"), None), P("groups", None, None, None)),
        check_vma=False,
    )
```

```python
import functools

import jax
import jax.numpy as jnp
from jax import lax
from jax.experimental import pallas as pl
from jax.experimental.pallas import tpu as pltpu
from jax.sharding import PartitionSpec as P

BLK = 128
PIECES = 4
DIRECT = (0,)
ORDER = ()
MESH = pl.DeviceIdType.MESH


def split(x):
    high = x.astype(jnp.bfloat16)
    return high, (x - high.astype(jnp.float32)).astype(jnp.bfloat16)


def product(a, b):
    dot = functools.partial(jnp.dot, preferred_element_type=jnp.float32)
    return dot(a[0], b[0]) + (dot(a[0], b[1]) + dot(a[1], b[0]))


def pair_at(first, second):
    return second * (second + 1) // 2 + first


def log2(n):
    return n.bit_length() - 1


class Plan:
    def __init__(self, n_prow, count, width):
        self.bits = log2(n_prow)
        self.blocks = [(first, node) for node in reversed(range(count)) for first in range(node + 1)]
        self.chunks = range(len(self.blocks))
        self.base = [pair_at(*block) * width for block in self.blocks]
        self.width = width
        self.piece = width // n_prow
        self.rows = len(self.blocks) * width

    def half(self, bit):
        return self.width // 2 ** (bit + 1)


def kernel(
    n_prow, n_pcol, plan, readers_ref, a_hbm, f_hbm, win_hbm, diag_hbm, panels_hbm, pairs_hbm,
    a_ref, f_ref, win_ref, diag_ref, v_ref, ath_ref, atl_ref, vh_ref, vl_ref,
    wh_ref, wl_ref, dh_ref, dl_ref, x_ref, s_ref, panel_ref,
    line_ref, turn_ref, y_ref, sum_ref, final_ref, fold_ref, middle_ref, direct_ref,
    load_sem, panel_sem, pairs_sem, line_send, line_recv,
    turn_send, turn_recv, y_send, y_recv, w_send, w_recv, back_send, back_recv, z_send, z_recv, direct_send, direct_recv,
    *more_refs,
):
    loads = [
        pltpu.make_async_copy(source, target, load_sem.at[at])
        for at, (source, target) in enumerate(
            [(f_hbm, f_ref), (a_hbm, a_ref), (diag_hbm, diag_ref), (win_hbm, win_ref)]
        )
    ]
    for load in loads:
        load.start()
    count, fine, width = f_ref.shape
    per_column = n_prow // n_pcol
    quarter = fine // PIECES
    bits = log2(n_prow)
    turn_in = more_refs[:bits]
    half_refs = more_refs[bits:]
    p = lax.axis_index("prow")
    z = lax.axis_index("pcol")
    order = list(reversed(range(count)))
    chunks_of = {node: [c for c in plan.chunks if plan.blocks[c][1] == node] for node in order}

    barrier = pltpu.get_barrier_semaphore()

    def greet(dest):
        pl.semaphore_signal(barrier, inc=1, device_id=dest, device_id_type=MESH)

    @pl.when(z > 0)
    def _():
        greet({"prow": p, "pcol": z - 1})

    @pl.when(z < n_pcol - 1)
    def _():
        greet({"prow": p, "pcol": z + 1})

    for bit in range(bits):
        greet({"prow": p + (1 - (p // 2**bit) % 2 * 2) * 2**bit, "pcol": z})
    greeted = bits + jnp.where(z > 0, 1, 0) + jnp.where(z < n_pcol - 1, 1, 0)

    reader = readers_ref[(p * n_pcol + z) * fine // BLK]
    masks = [jnp.where(reader <= node, 1.0, 0.0).astype(jnp.float32) for node in range(count)]

    def rows(start, size):
        return pl.ds(start if isinstance(start, int) else pl.multiple_of(start, 8), size)

    share = v_ref.shape[1] - fine
    unit_row = lax.broadcasted_iota(jnp.int32, (share, width), 0) + (p * n_pcol + z) * share
    unit_col = lax.broadcasted_iota(jnp.int32, (share, width), 1)

    def win_at(first, second):
        at = second * (second - 1) // 2 + first
        return wh_ref[at], wl_ref[at]

    def diag_at(node):
        return dh_ref[node], dl_ref[node]

    def split_factors():
        loads[2].wait()
        loads[3].wait()
        for node in range(count):
            dh_ref[node], dl_ref[node] = split(diag_ref[node])
        for at in range(win_ref.shape[0]):
            wh_ref[at], wl_ref[at] = split(win_ref[at])

    def local_v(node):
        units = jnp.where(unit_row == unit_col + node * width, 1.0, 0.0).astype(jnp.float32)
        total = jnp.concatenate([f_ref[node], units], axis=0)
        for other in range(node + 1, count):
            total = total - product(split(v_ref[other]), win_at(node, other))
        v = product(split(total), diag_at(node))
        v_ref[node] = v
        vh_ref[node], vl_ref[node] = split(v.T)

    def before_x(node):
        total = jnp.zeros((fine, width), jnp.float32)
        for other in range(node + 1, count):
            total = total + product(split(x_ref[other]), win_at(node, other))
        s_ref[node] = total

    def panel_copy(node):
        return pltpu.make_async_copy(panel_ref.at[node], panels_hbm.at[node], panel_sem.at[node])

    def window_part(node, y):
        x = product(split(y - s_ref[node]), diag_at(node))
        x_ref[node] = x
        ends = split(jnp.concatenate([x, v_ref[node, pl.ds(fine, share)]], axis=0))
        for other in range(node + 1):
            sum_ref[pl.ds(pair_at(other, node) * width, width)] = product((vh_ref[other], vl_ref[other]), ends)
        panel_ref[node] = -x * masks[node]
        panel_copy(node).start()

    middle = n_pcol // 2
    lower = z < middle
    beyond = jnp.where(lower, middle, middle - 1)
    toward = jnp.where(lower, z + 1, z - 1)
    outward = jnp.where(lower, z - 1, z + 1)
    depth = jnp.where(lower, z, n_pcol - 1 - z)
    relays = depth == middle - 1

    def line_copy(node, origin, dest, sem):
        return pltpu.make_async_remote_copy(
            src_ref=line_ref.at[node, origin],
            dst_ref=line_ref.at[node, origin],
            send_sem=sem,
            recv_sem=line_recv.at[node, origin],
            device_id={"prow": p, "pcol": dest},
            device_id_type=MESH,
        )

    def line_side(side, back):
        return z - back if side == 0 else z + back

    def line_sends(side, hop):
        if side == 0:
            return jnp.logical_and(z >= hop, z < n_pcol - 1)
        return jnp.logical_and(z + hop < n_pcol, z > 0)

    def line_gets(side, hop):
        return z - 1 - hop >= 0 if side == 0 else z + 1 + hop < n_pcol

    def line_step(node, hop):
        for side in (0, 1):
            if hop > 0:
                @pl.when(line_gets(side, hop - 1))
                def _():
                    line_copy(node, line_side(side, hop), line_side(side, 1), line_send.at[node, side, hop - 1]).wait_recv()

            if hop < n_pcol - 1:
                @pl.when(line_sends(side, hop))
                def _():
                    line_copy(node, line_side(side, hop), line_side(side, -1), line_send.at[node, side, hop]).start()

    def line_finish(node):
        for hop in range(n_pcol - 1):
            for side in (0, 1):
                @pl.when(line_sends(side, hop))
                def _():
                    line_copy(node, line_side(side, hop), line_side(side, -1), line_send.at[node, side, hop]).wait_send()

    def split_turned():
        loads[1].wait()
        turned = split(a_ref[...].T)
        for group in range(n_prow // PIECES):
            for owner in range(PIECES):
                for chunk in range(PIECES):
                    at = (group * PIECES + owner) * fine + chunk * quarter
                    to = (group * PIECES + chunk) * fine + owner * quarter
                    ath_ref[pl.ds(to, quarter)] = turned[0][at : at + quarter]
                    atl_ref[pl.ds(to, quarter)] = turned[1][at : at + quarter]

    turn_starts = [0]
    for bit in range(bits):
        turn_starts.append(turn_starts[bit] + (p // 2**bit) % 2 * (n_prow // 2 ** (bit + 1)))
    slot = turn_starts[bits]

    def mate(axis, bit):
        if axis == "prow":
            return {"prow": p + (1 - (p // 2**bit) % 2 * 2) * 2**bit, "pcol": z}
        return {"prow": p, "pcol": z + (1 - (z // 2**bit) % 2 * 2) * 2**bit}

    def turn_copy(node, bit):
        half = n_prow // 2 ** (bit + 1)
        away = turn_starts[bit] + (1 - (p // 2**bit) % 2) * half
        return pltpu.make_async_remote_copy(
            src_ref=turn_ref.at[node, pl.ds(away, half)],
            dst_ref=turn_in[bit].at[node],
            send_sem=turn_send.at[node, bit],
            recv_sem=turn_recv.at[node, bit],
            device_id=mate("prow", bit),
            device_id_type=MESH,
        )

    def turn_multiply(node):
        gathered = line_ref[node].reshape(a_ref.shape[0], width)
        result = product((ath_ref[...], atl_ref[...]), split(gathered))
        turn_ref[node] = result.reshape(n_prow, PIECES, quarter, width)
        turn_copy(node, 0).start()

    def y_copy(node, owner):
        place = slot // PIECES * PIECES + owner
        return pltpu.make_async_remote_copy(
            src_ref=turn_ref.at[node, slot, owner],
            dst_ref=y_ref.at[node, slot % PIECES],
            send_sem=y_send.at[node, owner],
            recv_sem=y_recv.at[node],
            device_id={"prow": z * per_column + place // n_pcol, "pcol": place % n_pcol},
            device_id_type=MESH,
        )

    def y_mine(owner):
        place = slot // PIECES * PIECES + owner
        return jnp.logical_and(z * per_column + place // n_pcol == p, place % n_pcol == z)

    def turn_step(node, bit):
        turn_copy(node, bit).wait_recv()
        mine = pl.ds(turn_starts[bit + 1], n_prow // 2 ** (bit + 1))
        turn_ref[node, mine] += turn_in[bit][node]
        if bit + 1 < bits:
            turn_copy(node, bit + 1).start()
            return
        for owner in range(PIECES):
            @pl.when(y_mine(owner))
            def _():
                pltpu.make_async_copy(
                    turn_ref.at[node, slot, owner], y_ref.at[node, slot % PIECES], y_recv.at[node]
                ).start()

            @pl.when(jnp.logical_not(y_mine(owner)))
            def _():
                y_copy(node, owner).start()

    def y_end(node):
        pltpu.make_async_copy(y_ref.at[node], y_ref.at[node], y_recv.at[node]).wait()

    def turn_finish(node):
        for bit in range(bits):
            turn_copy(node, bit).wait_send()
        for owner in range(PIECES):
            @pl.when(jnp.logical_not(y_mine(owner)))
            def _():
                y_copy(node, owner).wait_send()

    starts = [0]
    for bit in range(bits):
        starts.append(starts[bit] + (p // 2**bit) % 2 * plan.half(bit))

    def piece_rows(chunk):
        return rows(plan.base[chunk] + starts[bits], plan.piece)

    def chunk_rows(chunk, size):
        return pl.ds(chunk * size, size)

    def w_copy(chunk, bit):
        half = plan.half(bit)
        away = plan.base[chunk] + starts[bit] + (1 - (p // 2**bit) % 2) * half
        return pltpu.make_async_remote_copy(
            src_ref=sum_ref.at[rows(away, half)],
            dst_ref=half_refs[bit].at[chunk_rows(chunk, half)],
            send_sem=w_send.at[chunk, bit],
            recv_sem=w_recv.at[chunk, bit],
            device_id=mate("prow", bit),
            device_id_type=MESH,
        )

    def z_copy(chunk, kind, dest):
        source_ref = final_ref if kind == 2 else sum_ref
        target_ref = (fold_ref, middle_ref)[kind].at[chunk_rows(chunk, plan.piece)] if kind < 2 else None
        return pltpu.make_async_remote_copy(
            src_ref=source_ref.at[piece_rows(chunk)],
            dst_ref=final_ref.at[piece_rows(chunk)] if kind == 2 else target_ref,
            send_sem=z_send.at[chunk, kind],
            recv_sem=z_recv.at[chunk, kind],
            device_id={"prow": p, "pcol": dest},
            device_id_type=MESH,
        )

    def back_copy(chunk, bit):
        part = rows(plan.base[chunk] + starts[bit + 1], plan.half(bit))
        return pltpu.make_async_remote_copy(
            src_ref=final_ref.at[part],
            dst_ref=final_ref.at[part],
            send_sem=back_send.at[chunk, bit],
            recv_sem=back_recv.at[chunk, bit],
            device_id=mate("prow", bit),
            device_id_type=MESH,
        )

    def pairs_copy(chunk):
        part = pl.ds(plan.base[chunk], width)
        return pltpu.make_async_copy(final_ref.at[part], pairs_hbm.at[part], pairs_sem.at[chunk])

    members = n_prow // 2 * n_pcol
    member = p // 2 * n_pcol + z
    small = plan.half(0) // members
    direct = [c for c in plan.chunks if plan.blocks[c][1] in DIRECT and small % 8 == 0]

    def member_rows(chunk, at):
        return rows(plan.base[chunk] + starts[1] + at * small, small)

    def member_copy(chunk, kind, sender, dest):
        place = direct.index(chunk)
        if kind == 0:
            source_ref, target_ref = sum_ref.at[member_rows(chunk, dest)], direct_ref.at[place, sender]
        else:
            source_ref = target_ref = final_ref.at[member_rows(chunk, sender)]
        return pltpu.make_async_remote_copy(
            src_ref=source_ref,
            dst_ref=target_ref,
            send_sem=direct_send.at[place, kind, dest],
            recv_sem=direct_recv.at[place, kind, sender],
            device_id={"prow": dest // n_pcol * 2 + p % 2, "pcol": dest % n_pcol},
            device_id_type=MESH,
        )

    def members_but(run):
        for at in range(members):
            @pl.when(member != at)
            def _():
                run(at)

    def direct_start(chunk):
        w_copy(chunk, 0).wait_recv()
        half = plan.half(0)
        mine = rows(plan.base[chunk] + starts[1], half)
        sum_ref[mine] += half_refs[0][chunk_rows(chunk, half)]
        members_but(lambda at: member_copy(chunk, 0, member, at).start())

    def direct_sum(chunk):
        place = direct.index(chunk)
        direct_ref[place, member] = sum_ref[member_rows(chunk, member)]
        members_but(lambda at: member_copy(chunk, 0, at, at).wait_recv())
        total = direct_ref[place, 0]
        for at in range(1, members):
            total = total + direct_ref[place, at]
        final_ref[member_rows(chunk, member)] = total
        members_but(lambda at: member_copy(chunk, 1, member, at).start())

    def direct_end(chunk):
        members_but(lambda at: member_copy(chunk, 1, at, at).wait_recv())
        back_copy(chunk, 0).start()

    def direct_finish(chunk):
        w_copy(chunk, 0).wait_send()
        back_copy(chunk, 0).wait_send()
        for kind in (0, 1):
            members_but(lambda at: member_copy(chunk, kind, member, at).wait_send())
        pairs_copy(chunk).wait()

    def inward(chunk):
        @pl.when(depth < middle - 1)
        def _():
            z_copy(chunk, 0, toward).start()

        @pl.when(relays)
        def _():
            z_copy(chunk, 1, toward).start()

    def w_step(chunk, bit):
        w_copy(chunk, bit).wait_recv()
        half = plan.half(bit)
        mine = rows(plan.base[chunk] + starts[bit + 1], half)
        sum_ref[mine] += half_refs[bit][chunk_rows(chunk, half)]
        if bit + 1 < bits:
            w_copy(chunk, bit + 1).start()
        else:
            @pl.when(depth == 0)
            def _():
                inward(chunk)

    def fold_step(chunk, step):
        @pl.when(depth == step)
        def _():
            z_copy(chunk, 0, outward).wait_recv()
            sum_ref[piece_rows(chunk)] += fold_ref[chunk_rows(chunk, plan.piece)]
            inward(chunk)

    def outgoing(chunk):
        @pl.when(depth > 0)
        def _():
            z_copy(chunk, 2, outward).start()

        back_copy(chunk, bits - 1).start()

    def middle_step(chunk):
        @pl.when(relays)
        def _():
            z_copy(chunk, 1, toward).wait_recv()
            final_ref[piece_rows(chunk)] = sum_ref[piece_rows(chunk)] + middle_ref[chunk_rows(chunk, plan.piece)]
            outgoing(chunk)

    def unfold_step(chunk, step):
        @pl.when(depth == step)
        def _():
            z_copy(chunk, 2, toward).wait_recv()
            outgoing(chunk)

    def back_step(chunk, bit):
        back_copy(chunk, bit).wait_recv()
        if bit > 0:
            back_copy(chunk, bit - 1).start()
        else:
            pairs_copy(chunk).start()

    def window_finish(chunk):
        for bit in range(bits):
            w_copy(chunk, bit).wait_send()
            back_copy(chunk, bit).wait_send()

        @pl.when(depth < middle - 1)
        def _():
            z_copy(chunk, 0, toward).wait_send()

        @pl.when(relays)
        def _():
            z_copy(chunk, 1, toward).wait_send()

        @pl.when(depth > 0)
        def _():
            z_copy(chunk, 2, outward).wait_send()

        pairs_copy(chunk).wait()

    def close(node):
        window_part(node, y_ref[node].reshape(fine, width))
        for chunk in chunks_of[node]:
            w_copy(chunk, 0).start()

    def prepare(node):
        f_ref[node] = f_ref[node] * masks[node]
        line_ref[node, z] = f_ref[node]

    stages, due = {}, {}

    def at(time, name, run, *args):
        stages[name] = functools.partial(run, *args)
        due[name] = (time, len(due))

    at(0.0, ("bar",), pl.semaphore_wait, barrier, greeted)
    for node in order[1:]:
        at(0.2, ("p", node), prepare, node)
    at(0.3, ("st",), split_turned)
    at(1.0, ("sf",), split_factors)
    latest = 0.0
    for turn, node in enumerate(order):
        at(5.0 + turn, ("v", node), local_v, node)
        start = 8.0 * turn
        hops = n_pcol - 1
        at(0.1 + start, ("l", node, 0), line_step, node, 0)
        for hop in range(1, hops + 1):
            at(0.1 + start + 5.0 * hop, ("l", node, hop), line_step, node, hop)
        done = 0.2 + start + 5.0 * hops
        at(done, ("tm", node), turn_multiply, node)
        for bit in range(bits):
            done += 2.0 if bit == 0 else 5.0
            at(done, ("t", node, bit), turn_step, node, bit)
        latest = max(done + 5.0, latest + 2.0)
        at(latest - 1.0, ("b", node), before_x, node)
        at(latest, ("y", node), y_end, node)
        at(latest, ("x", node), close, node)
        for turn_w, chunk in enumerate(chunks_of[node]):
            time = latest + 2.0 * turn_w
            if chunk in direct:
                at(time + 2.0, ("w", chunk, 0), direct_start, chunk)
                at(time + 8.0, ("d", chunk, 0), direct_sum, chunk)
                at(time + 14.0, ("d", chunk, 1), direct_end, chunk)
                at(time + 16.0, ("k", chunk, 0), back_step, chunk, 0)
                continue
            for bit in range(bits):
                time += 2.0 if bit == 0 else 4.0
                at(time, ("w", chunk, bit), w_step, chunk, bit)
            for step in range(1, middle):
                time += 4.0
                at(time, ("w", chunk, bits + step - 1), fold_step, chunk, step)
            time += 4.0
            at(time, ("w", chunk, bits + middle - 1), middle_step, chunk)
            for step in reversed(range(middle - 1)):
                time += 4.0
                at(time, ("k", chunk, bits + step), unfold_step, chunk, step)
            for bit in reversed(range(bits)):
                time += 4.0 if bit else 2.0
                at(time, ("k", chunk, bit), back_step, chunk, bit)

    sequence = ORDER if set(ORDER) == set(stages) else sorted(stages, key=due.get)
    loads[0].wait()
    prepare(order[0])
    for name in sequence:
        stages[name]()
    for node in order:
        line_finish(node)
        turn_finish(node)
        panel_copy(node).wait()
    for chunk in plan.chunks:
        (direct_finish if chunk in direct else window_finish)(chunk)


def assemble_kernel(panels_in, pairs_in, panels_out, window_out, panel_ref, pairs_ref, turned_ref, in_sem, out_sem):
    count, _, width = panels_in.shape
    into = pltpu.make_async_copy(panels_in, panel_ref, in_sem.at[0])
    into.start()
    order = [(first, second) for second in reversed(range(count)) for first in range(second + 1)]

    def load(first, second):
        at = pair_at(first, second)
        return pltpu.make_async_copy(pairs_in.at[pl.ds(at * width, width)], pairs_ref.at[at], in_sem.at[1 + at])

    for first, second in order:
        load(first, second).start()
    stores = []
    for first, second in order:
        at = pair_at(first, second)
        load(first, second).wait()
        stores.append(pltpu.make_async_copy(pairs_ref.at[at], window_out.at[first, second], out_sem.at[1 + len(stores)]))
        stores[-1].start()
        if first != second:
            turned_ref[at] = pairs_ref[at].T
            stores.append(
                pltpu.make_async_copy(turned_ref.at[at], window_out.at[second, first], out_sem.at[1 + len(stores)])
            )
            stores[-1].start()
    into.wait()
    stores.append(pltpu.make_async_copy(panel_ref, panels_out, out_sem.at[0]))
    stores[-1].start()
    for store in stores:
        store.wait()


def sweep(n_prow, n_pcol, readers, anc_inverse, anc_factor, win_factor, diag_inverse):
    count, fine, width = anc_factor.shape
    pairs = count * (count + 1) // 2
    share = count * width // (n_prow * n_pcol)
    bits = log2(n_prow)
    quarter = fine // PIECES
    plan = Plan(n_prow, count, width)
    chunks = len(plan.chunks)
    members = n_prow // 2 * n_pcol
    block_rows, block_cols = anc_inverse.shape
    hbm = pl.BlockSpec(memory_space=pltpu.HBM)
    operands = (anc_inverse, anc_factor, win_factor, diag_inverse)
    f32, b16 = jnp.float32, jnp.bfloat16
    dma = pltpu.SemaphoreType.DMA
    panels, blocks = pl.pallas_call(
        functools.partial(kernel, n_prow, n_pcol, plan),
        out_shape=(
            jax.ShapeDtypeStruct((count, fine, width), f32),
            jax.ShapeDtypeStruct((pairs * width, width), f32),
        ),
        in_specs=[pl.BlockSpec(memory_space=pltpu.SMEM)] + [hbm] * 4,
        out_specs=(hbm, hbm),
        scratch_shapes=[pltpu.VMEM(operand.shape, f32) for operand in operands]
        + [
            pltpu.VMEM((count, fine + share, width), f32),
            pltpu.VMEM((block_cols, block_rows), b16),
            pltpu.VMEM((block_cols, block_rows), b16),
            pltpu.VMEM((count, width, fine + share), b16),
            pltpu.VMEM((count, width, fine + share), b16),
            pltpu.VMEM(win_factor.shape, b16),
            pltpu.VMEM(win_factor.shape, b16),
            pltpu.VMEM(diag_inverse.shape, b16),
            pltpu.VMEM(diag_inverse.shape, b16),
            pltpu.VMEM((count, fine, width), f32),
            pltpu.VMEM((count, fine, width), f32),
            pltpu.VMEM((count, fine, width), f32),
            pltpu.VMEM((count, n_pcol, fine, width), f32),
            pltpu.VMEM((count, n_prow, PIECES, quarter, width), f32),
            pltpu.VMEM((count, PIECES, quarter, width), f32),
            pltpu.VMEM((plan.rows, width), f32),
            pltpu.VMEM((plan.rows, width), f32),
            pltpu.VMEM((chunks * plan.piece, width), f32),
            pltpu.VMEM((chunks * plan.piece, width), f32),
            pltpu.VMEM((sum(DIRECT) + len(DIRECT), members, max(8, width // 2 // members), width), f32),
            dma((len(operands),)),
            dma((count,)),
            dma((chunks,)),
            dma((count, 2, n_pcol)),
            dma((count, n_pcol)),
            dma((count, bits)),
            dma((count, bits)),
            dma((count, PIECES)),
            dma((count,)),
            dma((chunks, bits)),
            dma((chunks, bits)),
            dma((chunks, bits)),
            dma((chunks, bits)),
            dma((chunks, 3)),
            dma((chunks, 3)),
            dma((sum(DIRECT) + len(DIRECT), 2, members)),
            dma((sum(DIRECT) + len(DIRECT), 2, members)),
        ]
        + [pltpu.VMEM((count, n_prow // 2 ** (bit + 1), PIECES, quarter, width), f32) for bit in range(bits)]
        + [pltpu.VMEM((chunks * plan.half(bit), width), f32) for bit in range(bits)],
        compiler_params=pltpu.CompilerParams(
            collective_id=0, has_side_effects=True, vmem_limit_bytes=58 * 2**20
        ),
    )(readers, *operands)
    return pl.pallas_call(
        assemble_kernel,
        out_shape=(
            jax.ShapeDtypeStruct((count, fine, width), f32),
            jax.ShapeDtypeStruct((count, count, width, width), f32),
        ),
        in_specs=[hbm, hbm],
        out_specs=(hbm, hbm),
        scratch_shapes=[
            pltpu.VMEM((count, fine, width), f32),
            pltpu.VMEM((pairs, width, width), f32),
            pltpu.VMEM((pairs, width, width), f32),
            dma((1 + pairs,)),
            dma((1 + count * count,)),
        ],
        compiler_params=pltpu.CompilerParams(vmem_limit_bytes=60 * 2**20),
    )(panels, blocks)


def per_device(anc_inverse, anc_factor, win_factor, diag_inverse, first_reader):
    n_prow = lax.axis_size("prow")
    n_pcol = lax.axis_size("pcol")
    return sweep(n_prow, n_pcol, first_reader, anc_inverse, anc_factor, win_factor, diag_inverse)


def solution(mesh):
    return jax.shard_map(
        per_device,
        mesh=mesh,
        in_specs=(
            P(("groups", "prow"), "pcol"),
            P("groups", ("prow", "pcol"), None),
            P("groups", None, None),
            P("groups", None, None),
            P("groups"),
        ),
        out_specs=(P("groups", ("prow", "pcol"), None), P("groups", None, None, None)),
        check_vma=False,
    )
```

```python
import functools

import jax
import jax.numpy as jnp
from jax import lax
from jax.experimental import pallas as pl
from jax.experimental.pallas import tpu as pltpu
from jax.sharding import PartitionSpec as P

BLK = 128
PIECES = 4
DIRECT = (0,)
ORDER = ()
MESH = pl.DeviceIdType.MESH


def split(x):
    high = x.astype(jnp.bfloat16)
    return high, (x - high.astype(jnp.float32)).astype(jnp.bfloat16)


def product(a, b):
    dot = functools.partial(jnp.dot, preferred_element_type=jnp.float32)
    return dot(a[0], b[0]) + (dot(a[0], b[1]) + dot(a[1], b[0]))


def pair_at(first, second):
    return second * (second + 1) // 2 + first


def log2(n):
    return n.bit_length() - 1


class Plan:
    def __init__(self, n_prow, count, width):
        self.bits = log2(n_prow)
        self.blocks = [(first, node) for node in reversed(range(count)) for first in range(node + 1)]
        self.chunks = range(len(self.blocks))
        self.base = [pair_at(*block) * width for block in self.blocks]
        self.width = width
        self.piece = width // n_prow
        self.rows = len(self.blocks) * width

    def half(self, bit):
        return self.width // 2 ** (bit + 1)


def kernel(
    n_prow, n_pcol, plan, readers_ref, a_hbm, f_hbm, win_hbm, diag_hbm, panels_hbm, pairs_hbm,
    a_ref, f_ref, win_ref, diag_ref, v_ref, ath_ref, atl_ref, vh_ref, vl_ref,
    wh_ref, wl_ref, dh_ref, dl_ref, x_ref, s_ref, panel_ref,
    line_ref, turn_ref, y_ref, sum_ref, final_ref, fold_ref, middle_ref, direct_ref,
    load_sem, panel_sem, pairs_sem, line_send, line_recv,
    turn_send, turn_recv, y_send, y_recv, w_send, w_recv, back_send, back_recv, z_send, z_recv, direct_send, direct_recv,
    *more_refs,
):
    loads = [
        pltpu.make_async_copy(source, target, load_sem.at[at])
        for at, (source, target) in enumerate(
            [(f_hbm, f_ref), (a_hbm, a_ref), (diag_hbm, diag_ref), (win_hbm, win_ref)]
        )
    ]
    for load in loads:
        load.start()
    count, fine, width = f_ref.shape
    per_column = n_prow // n_pcol
    quarter = fine // PIECES
    bits = log2(n_prow)
    turn_in = more_refs[:bits]
    half_refs = more_refs[bits:]
    p = lax.axis_index("prow")
    z = lax.axis_index("pcol")
    order = list(reversed(range(count)))
    chunks_of = {node: [c for c in plan.chunks if plan.blocks[c][1] == node] for node in order}

    barrier = pltpu.get_barrier_semaphore()

    def greet(dest):
        pl.semaphore_signal(barrier, inc=1, device_id=dest, device_id_type=MESH)

    @pl.when(z > 0)
    def _():
        greet({"prow": p, "pcol": z - 1})

    @pl.when(z < n_pcol - 1)
    def _():
        greet({"prow": p, "pcol": z + 1})

    for bit in range(bits):
        greet({"prow": p + (1 - (p // 2**bit) % 2 * 2) * 2**bit, "pcol": z})
    greeted = bits + jnp.where(z > 0, 1, 0) + jnp.where(z < n_pcol - 1, 1, 0)

    reader = readers_ref[(p * n_pcol + z) * fine // BLK]
    masks = [jnp.where(reader <= node, 1.0, 0.0).astype(jnp.float32) for node in range(count)]

    def rows(start, size):
        return pl.ds(start if isinstance(start, int) else pl.multiple_of(start, 8), size)

    share = v_ref.shape[1] - fine
    unit_row = lax.broadcasted_iota(jnp.int32, (share, width), 0) + (p * n_pcol + z) * share
    unit_col = lax.broadcasted_iota(jnp.int32, (share, width), 1)

    def win_at(first, second):
        at = second * (second - 1) // 2 + first
        return wh_ref[at], wl_ref[at]

    def diag_at(node):
        return dh_ref[node], dl_ref[node]

    def split_factors():
        loads[2].wait()
        loads[3].wait()
        for node in range(count):
            dh_ref[node], dl_ref[node] = split(diag_ref[node])
        for at in range(win_ref.shape[0]):
            wh_ref[at], wl_ref[at] = split(win_ref[at])

    def local_v(node):
        units = jnp.where(unit_row == unit_col + node * width, 1.0, 0.0).astype(jnp.float32)
        total = jnp.concatenate([f_ref[node], units], axis=0)
        for other in range(node + 1, count):
            total = total - product(split(v_ref[other]), win_at(node, other))
        v = product(split(total), diag_at(node))
        v_ref[node] = v
        vh_ref[node], vl_ref[node] = split(v.T)

    def before_x(node):
        total = jnp.zeros((fine, width), jnp.float32)
        for other in range(node + 1, count):
            total = total + product(split(x_ref[other]), win_at(node, other))
        s_ref[node] = total

    def panel_copy(node):
        return pltpu.make_async_copy(panel_ref.at[node], panels_hbm.at[node], panel_sem.at[node])

    def window_part(node, y):
        x = product(split(y - s_ref[node]), diag_at(node))
        x_ref[node] = x
        ends = split(jnp.concatenate([x, v_ref[node, pl.ds(fine, share)]], axis=0))
        for other in range(node + 1):
            sum_ref[pl.ds(pair_at(other, node) * width, width)] = product((vh_ref[other], vl_ref[other]), ends)
        panel_ref[node] = -x * masks[node]
        panel_copy(node).start()

    middle = n_pcol // 2
    lower = z < middle
    beyond = jnp.where(lower, middle, middle - 1)
    toward = jnp.where(lower, z + 1, z - 1)
    outward = jnp.where(lower, z - 1, z + 1)
    depth = jnp.where(lower, z, n_pcol - 1 - z)
    relays = depth == middle - 1

    def line_copy(node, origin, dest, sem):
        return pltpu.make_async_remote_copy(
            src_ref=line_ref.at[node, origin],
            dst_ref=line_ref.at[node, origin],
            send_sem=sem,
            recv_sem=line_recv.at[node, origin],
            device_id={"prow": p, "pcol": dest},
            device_id_type=MESH,
        )

    def line_side(side, back):
        return z - back if side == 0 else z + back

    def line_sends(side, hop):
        if side == 0:
            return jnp.logical_and(z >= hop, z < n_pcol - 1)
        return jnp.logical_and(z + hop < n_pcol, z > 0)

    def line_gets(side, hop):
        return z - 1 - hop >= 0 if side == 0 else z + 1 + hop < n_pcol

    def line_step(node, hop):
        for side in (0, 1):
            if hop > 0:
                @pl.when(line_gets(side, hop - 1))
                def _():
                    line_copy(node, line_side(side, hop), line_side(side, 1), line_send.at[node, side, hop - 1]).wait_recv()

            if hop < n_pcol - 1:
                @pl.when(line_sends(side, hop))
                def _():
                    line_copy(node, line_side(side, hop), line_side(side, -1), line_send.at[node, side, hop]).start()

    def line_finish(node):
        for hop in range(n_pcol - 1):
            for side in (0, 1):
                @pl.when(line_sends(side, hop))
                def _():
                    line_copy(node, line_side(side, hop), line_side(side, -1), line_send.at[node, side, hop]).wait_send()

    def split_turned():
        loads[1].wait()
        turned = split(a_ref[...].T)
        for group in range(n_prow // PIECES):
            for owner in range(PIECES):
                for chunk in range(PIECES):
                    at = (group * PIECES + owner) * fine + chunk * quarter
                    to = (group * PIECES + chunk) * fine + owner * quarter
                    ath_ref[pl.ds(to, quarter)] = turned[0][at : at + quarter]
                    atl_ref[pl.ds(to, quarter)] = turned[1][at : at + quarter]

    turn_starts = [0]
    for bit in range(bits):
        turn_starts.append(turn_starts[bit] + (p // 2**bit) % 2 * (n_prow // 2 ** (bit + 1)))
    slot = turn_starts[bits]

    def mate(axis, bit):
        if axis == "prow":
            return {"prow": p + (1 - (p // 2**bit) % 2 * 2) * 2**bit, "pcol": z}
        return {"prow": p, "pcol": z + (1 - (z // 2**bit) % 2 * 2) * 2**bit}

    def turn_copy(node, bit):
        half = n_prow // 2 ** (bit + 1)
        away = turn_starts[bit] + (1 - (p // 2**bit) % 2) * half
        return pltpu.make_async_remote_copy(
            src_ref=turn_ref.at[node, pl.ds(away, half)],
            dst_ref=turn_in[bit].at[node],
            send_sem=turn_send.at[node, bit],
            recv_sem=turn_recv.at[node, bit],
            device_id=mate("prow", bit),
            device_id_type=MESH,
        )

    def turn_multiply(node):
        gathered = line_ref[node].reshape(a_ref.shape[0], width)
        result = product((ath_ref[...], atl_ref[...]), split(gathered))
        turn_ref[node] = result.reshape(n_prow, PIECES, quarter, width)
        turn_copy(node, 0).start()

    def y_copy(node, owner):
        place = slot // PIECES * PIECES + owner
        return pltpu.make_async_remote_copy(
            src_ref=turn_ref.at[node, slot, owner],
            dst_ref=y_ref.at[node, slot % PIECES],
            send_sem=y_send.at[node, owner],
            recv_sem=y_recv.at[node],
            device_id={"prow": z * per_column + place // n_pcol, "pcol": place % n_pcol},
            device_id_type=MESH,
        )

    def y_mine(owner):
        place = slot // PIECES * PIECES + owner
        return jnp.logical_and(z * per_column + place // n_pcol == p, place % n_pcol == z)

    def turn_step(node, bit):
        turn_copy(node, bit).wait_recv()
        mine = pl.ds(turn_starts[bit + 1], n_prow // 2 ** (bit + 1))
        turn_ref[node, mine] += turn_in[bit][node]
        if bit + 1 < bits:
            turn_copy(node, bit + 1).start()
            return
        for owner in range(PIECES):
            @pl.when(y_mine(owner))
            def _():
                pltpu.make_async_copy(
                    turn_ref.at[node, slot, owner], y_ref.at[node, slot % PIECES], y_recv.at[node]
                ).start()

            @pl.when(jnp.logical_not(y_mine(owner)))
            def _():
                y_copy(node, owner).start()

    def y_end(node):
        pltpu.make_async_copy(y_ref.at[node], y_ref.at[node], y_recv.at[node]).wait()

    def turn_finish(node):
        for bit in range(bits):
            turn_copy(node, bit).wait_send()
        for owner in range(PIECES):
            @pl.when(jnp.logical_not(y_mine(owner)))
            def _():
                y_copy(node, owner).wait_send()

    starts = [0]
    for bit in range(bits):
        starts.append(starts[bit] + (p // 2**bit) % 2 * plan.half(bit))

    def piece_rows(chunk):
        return rows(plan.base[chunk] + starts[bits], plan.piece)

    def chunk_rows(chunk, size):
        return pl.ds(chunk * size, size)

    def w_copy(chunk, bit):
        half = plan.half(bit)
        away = plan.base[chunk] + starts[bit] + (1 - (p // 2**bit) % 2) * half
        return pltpu.make_async_remote_copy(
            src_ref=sum_ref.at[rows(away, half)],
            dst_ref=half_refs[bit].at[chunk_rows(chunk, half)],
            send_sem=w_send.at[chunk, bit],
            recv_sem=w_recv.at[chunk, bit],
            device_id=mate("prow", bit),
            device_id_type=MESH,
        )

    def z_copy(chunk, kind, dest):
        source_ref = final_ref if kind == 2 else sum_ref
        target_ref = (fold_ref, middle_ref)[kind].at[chunk_rows(chunk, plan.piece)] if kind < 2 else None
        return pltpu.make_async_remote_copy(
            src_ref=source_ref.at[piece_rows(chunk)],
            dst_ref=final_ref.at[piece_rows(chunk)] if kind == 2 else target_ref,
            send_sem=z_send.at[chunk, kind],
            recv_sem=z_recv.at[chunk, kind],
            device_id={"prow": p, "pcol": dest},
            device_id_type=MESH,
        )

    def back_copy(chunk, bit):
        part = rows(plan.base[chunk] + starts[bit + 1], plan.half(bit))
        return pltpu.make_async_remote_copy(
            src_ref=final_ref.at[part],
            dst_ref=final_ref.at[part],
            send_sem=back_send.at[chunk, bit],
            recv_sem=back_recv.at[chunk, bit],
            device_id=mate("prow", bit),
            device_id_type=MESH,
        )

    def pairs_copy(chunk):
        part = pl.ds(plan.base[chunk], width)
        return pltpu.make_async_copy(final_ref.at[part], pairs_hbm.at[part], pairs_sem.at[chunk])

    members = n_prow // 2 * n_pcol
    member = p // 2 * n_pcol + z
    small = plan.half(0) // members
    direct = [c for c in plan.chunks if plan.blocks[c][1] in DIRECT and small % 8 == 0]

    def member_rows(chunk, at):
        return rows(plan.base[chunk] + starts[1] + at * small, small)

    def member_copy(chunk, kind, sender, dest):
        place = direct.index(chunk)
        if kind == 0:
            source_ref, target_ref = sum_ref.at[member_rows(chunk, dest)], direct_ref.at[place, sender]
        else:
            source_ref = target_ref = final_ref.at[member_rows(chunk, sender)]
        return pltpu.make_async_remote_copy(
            src_ref=source_ref,
            dst_ref=target_ref,
            send_sem=direct_send.at[place, kind, dest],
            recv_sem=direct_recv.at[place, kind, sender],
            device_id={"prow": dest // n_pcol * 2 + p % 2, "pcol": dest % n_pcol},
            device_id_type=MESH,
        )

    def members_but(run):
        for at in range(members):
            @pl.when(member != at)
            def _():
                run(at)

    def direct_start(chunk):
        w_copy(chunk, 0).wait_recv()
        half = plan.half(0)
        mine = rows(plan.base[chunk] + starts[1], half)
        sum_ref[mine] += half_refs[0][chunk_rows(chunk, half)]
        members_but(lambda at: member_copy(chunk, 0, member, at).start())

    def direct_sum(chunk):
        place = direct.index(chunk)
        direct_ref[place, member] = sum_ref[member_rows(chunk, member)]
        members_but(lambda at: member_copy(chunk, 0, at, at).wait_recv())
        total = direct_ref[place, 0]
        for at in range(1, members):
            total = total + direct_ref[place, at]
        final_ref[member_rows(chunk, member)] = total
        members_but(lambda at: member_copy(chunk, 1, member, at).start())

    def direct_end(chunk):
        members_but(lambda at: member_copy(chunk, 1, at, at).wait_recv())
        back_copy(chunk, 0).start()

    def direct_finish(chunk):
        w_copy(chunk, 0).wait_send()
        back_copy(chunk, 0).wait_send()
        for kind in (0, 1):
            members_but(lambda at: member_copy(chunk, kind, member, at).wait_send())
        pairs_copy(chunk).wait()

    def inward(chunk):
        @pl.when(depth < middle - 1)
        def _():
            z_copy(chunk, 0, toward).start()

        @pl.when(relays)
        def _():
            z_copy(chunk, 1, toward).start()

    def w_step(chunk, bit):
        w_copy(chunk, bit).wait_recv()
        half = plan.half(bit)
        mine = rows(plan.base[chunk] + starts[bit + 1], half)
        sum_ref[mine] += half_refs[bit][chunk_rows(chunk, half)]
        if bit + 1 < bits:
            w_copy(chunk, bit + 1).start()
        else:
            @pl.when(depth == 0)
            def _():
                inward(chunk)

    def fold_step(chunk, step):
        @pl.when(depth == step)
        def _():
            z_copy(chunk, 0, outward).wait_recv()
            sum_ref[piece_rows(chunk)] += fold_ref[chunk_rows(chunk, plan.piece)]
            inward(chunk)

    def outgoing(chunk):
        @pl.when(depth > 0)
        def _():
            z_copy(chunk, 2, outward).start()

        back_copy(chunk, bits - 1).start()

    def middle_step(chunk):
        @pl.when(relays)
        def _():
            z_copy(chunk, 1, toward).wait_recv()
            final_ref[piece_rows(chunk)] = sum_ref[piece_rows(chunk)] + middle_ref[chunk_rows(chunk, plan.piece)]
            outgoing(chunk)

    def unfold_step(chunk, step):
        @pl.when(depth == step)
        def _():
            z_copy(chunk, 2, toward).wait_recv()
            outgoing(chunk)

    def back_step(chunk, bit):
        back_copy(chunk, bit).wait_recv()
        if bit > 0:
            back_copy(chunk, bit - 1).start()
        else:
            pairs_copy(chunk).start()

    def window_finish(chunk):
        for bit in range(bits):
            w_copy(chunk, bit).wait_send()
            back_copy(chunk, bit).wait_send()

        @pl.when(depth < middle - 1)
        def _():
            z_copy(chunk, 0, toward).wait_send()

        @pl.when(relays)
        def _():
            z_copy(chunk, 1, toward).wait_send()

        @pl.when(depth > 0)
        def _():
            z_copy(chunk, 2, outward).wait_send()

        pairs_copy(chunk).wait()

    def close(node):
        window_part(node, y_ref[node].reshape(fine, width))
        for chunk in chunks_of[node]:
            w_copy(chunk, 0).start()

    def prepare(node):
        f_ref[node] = f_ref[node] * masks[node]
        line_ref[node, z] = f_ref[node]

    stages, due = {}, {}

    def at(time, name, run, *args):
        stages[name] = functools.partial(run, *args)
        due[name] = (time, len(due))

    at(0.0, ("bar",), pl.semaphore_wait, barrier, greeted)
    for node in order[1:]:
        at(0.2, ("p", node), prepare, node)
    at(0.3, ("st",), split_turned)
    at(1.0, ("sf",), split_factors)
    latest = 0.0
    for turn, node in enumerate(order):
        at(12.0 + 2.0 * turn, ("v", node), local_v, node)
        start = 8.0 * turn
        hops = n_pcol - 1
        at(0.1 + start, ("l", node, 0), line_step, node, 0)
        for hop in range(1, hops + 1):
            at(0.1 + start + 5.0 * hop, ("l", node, hop), line_step, node, hop)
        done = 0.2 + start + 5.0 * hops
        at(done, ("tm", node), turn_multiply, node)
        for bit in range(bits):
            done += 2.0 if bit == 0 else 5.0
            at(done, ("t", node, bit), turn_step, node, bit)
        latest = max(done + 5.0, latest + 2.0)
        at(latest - 1.0, ("b", node), before_x, node)
        at(latest, ("y", node), y_end, node)
        at(latest, ("x", node), close, node)
        for turn_w, chunk in enumerate(chunks_of[node]):
            time = latest + 2.0 * turn_w
            if chunk in direct:
                at(time + 2.0, ("w", chunk, 0), direct_start, chunk)
                at(time + 8.0, ("d", chunk, 0), direct_sum, chunk)
                at(time + 14.0, ("d", chunk, 1), direct_end, chunk)
                at(time + 16.0, ("k", chunk, 0), back_step, chunk, 0)
                continue
            for bit in range(bits):
                time += 2.0 if bit == 0 else 4.0
                at(time, ("w", chunk, bit), w_step, chunk, bit)
            for step in range(1, middle):
                time += 4.0
                at(time, ("w", chunk, bits + step - 1), fold_step, chunk, step)
            time += 4.0
            at(time, ("w", chunk, bits + middle - 1), middle_step, chunk)
            for step in reversed(range(middle - 1)):
                time += 4.0
                at(time, ("k", chunk, bits + step), unfold_step, chunk, step)
            for bit in reversed(range(bits)):
                time += 4.0 if bit else 2.0
                at(time, ("k", chunk, bit), back_step, chunk, bit)

    sequence = ORDER if set(ORDER) == set(stages) else sorted(stages, key=due.get)
    loads[0].wait()
    prepare(order[0])
    for name in sequence:
        stages[name]()
    for node in order:
        line_finish(node)
        turn_finish(node)
        panel_copy(node).wait()
    for chunk in plan.chunks:
        (direct_finish if chunk in direct else window_finish)(chunk)


def assemble_kernel(panels_in, pairs_in, panels_out, window_out, panel_ref, pairs_ref, turned_ref, in_sem, out_sem):
    count, _, width = panels_in.shape
    into = pltpu.make_async_copy(panels_in, panel_ref, in_sem.at[0])
    into.start()
    order = [(first, second) for second in reversed(range(count)) for first in range(second + 1)]

    def load(first, second):
        at = pair_at(first, second)
        return pltpu.make_async_copy(pairs_in.at[pl.ds(at * width, width)], pairs_ref.at[at], in_sem.at[1 + at])

    for first, second in order:
        load(first, second).start()
    stores = []
    for first, second in order:
        at = pair_at(first, second)
        load(first, second).wait()
        stores.append(pltpu.make_async_copy(pairs_ref.at[at], window_out.at[first, second], out_sem.at[1 + len(stores)]))
        stores[-1].start()
        if first != second:
            turned_ref[at] = pairs_ref[at].T
            stores.append(
                pltpu.make_async_copy(turned_ref.at[at], window_out.at[second, first], out_sem.at[1 + len(stores)])
            )
            stores[-1].start()
    into.wait()
    stores.append(pltpu.make_async_copy(panel_ref, panels_out, out_sem.at[0]))
    stores[-1].start()
    for store in stores:
        store.wait()


def sweep(n_prow, n_pcol, readers, anc_inverse, anc_factor, win_factor, diag_inverse):
    count, fine, width = anc_factor.shape
    pairs = count * (count + 1) // 2
    share = count * width // (n_prow * n_pcol)
    bits = log2(n_prow)
    quarter = fine // PIECES
    plan = Plan(n_prow, count, width)
    chunks = len(plan.chunks)
    members = n_prow // 2 * n_pcol
    block_rows, block_cols = anc_inverse.shape
    hbm = pl.BlockSpec(memory_space=pltpu.HBM)
    operands = (anc_inverse, anc_factor, win_factor, diag_inverse)
    f32, b16 = jnp.float32, jnp.bfloat16
    dma = pltpu.SemaphoreType.DMA
    panels, blocks = pl.pallas_call(
        functools.partial(kernel, n_prow, n_pcol, plan),
        out_shape=(
            jax.ShapeDtypeStruct((count, fine, width), f32),
            jax.ShapeDtypeStruct((pairs * width, width), f32),
        ),
        in_specs=[pl.BlockSpec(memory_space=pltpu.SMEM)] + [hbm] * 4,
        out_specs=(hbm, hbm),
        scratch_shapes=[pltpu.VMEM(operand.shape, f32) for operand in operands]
        + [
            pltpu.VMEM((count, fine + share, width), f32),
            pltpu.VMEM((block_cols, block_rows), b16),
            pltpu.VMEM((block_cols, block_rows), b16),
            pltpu.VMEM((count, width, fine + share), b16),
            pltpu.VMEM((count, width, fine + share), b16),
            pltpu.VMEM(win_factor.shape, b16),
            pltpu.VMEM(win_factor.shape, b16),
            pltpu.VMEM(diag_inverse.shape, b16),
            pltpu.VMEM(diag_inverse.shape, b16),
            pltpu.VMEM((count, fine, width), f32),
            pltpu.VMEM((count, fine, width), f32),
            pltpu.VMEM((count, fine, width), f32),
            pltpu.VMEM((count, n_pcol, fine, width), f32),
            pltpu.VMEM((count, n_prow, PIECES, quarter, width), f32),
            pltpu.VMEM((count, PIECES, quarter, width), f32),
            pltpu.VMEM((plan.rows, width), f32),
            pltpu.VMEM((plan.rows, width), f32),
            pltpu.VMEM((chunks * plan.piece, width), f32),
            pltpu.VMEM((chunks * plan.piece, width), f32),
            pltpu.VMEM((sum(DIRECT) + len(DIRECT), members, max(8, width // 2 // members), width), f32),
            dma((len(operands),)),
            dma((count,)),
            dma((chunks,)),
            dma((count, 2, n_pcol)),
            dma((count, n_pcol)),
            dma((count, bits)),
            dma((count, bits)),
            dma((count, PIECES)),
            dma((count,)),
            dma((chunks, bits)),
            dma((chunks, bits)),
            dma((chunks, bits)),
            dma((chunks, bits)),
            dma((chunks, 3)),
            dma((chunks, 3)),
            dma((sum(DIRECT) + len(DIRECT), 2, members)),
            dma((sum(DIRECT) + len(DIRECT), 2, members)),
        ]
        + [pltpu.VMEM((count, n_prow // 2 ** (bit + 1), PIECES, quarter, width), f32) for bit in range(bits)]
        + [pltpu.VMEM((chunks * plan.half(bit), width), f32) for bit in range(bits)],
        compiler_params=pltpu.CompilerParams(
            collective_id=0, has_side_effects=True, vmem_limit_bytes=58 * 2**20
        ),
    )(readers, *operands)
    return pl.pallas_call(
        assemble_kernel,
        out_shape=(
            jax.ShapeDtypeStruct((count, fine, width), f32),
            jax.ShapeDtypeStruct((count, count, width, width), f32),
        ),
        in_specs=[hbm, hbm],
        out_specs=(hbm, hbm),
        scratch_shapes=[
            pltpu.VMEM((count, fine, width), f32),
            pltpu.VMEM((pairs, width, width), f32),
            pltpu.VMEM((pairs, width, width), f32),
            dma((1 + pairs,)),
            dma((1 + count * count,)),
        ],
        compiler_params=pltpu.CompilerParams(vmem_limit_bytes=60 * 2**20),
    )(panels, blocks)


def per_device(anc_inverse, anc_factor, win_factor, diag_inverse, first_reader):
    n_prow = lax.axis_size("prow")
    n_pcol = lax.axis_size("pcol")
    return sweep(n_prow, n_pcol, first_reader, anc_inverse, anc_factor, win_factor, diag_inverse)


def solution(mesh):
    return jax.shard_map(
        per_device,
        mesh=mesh,
        in_specs=(
            P(("groups", "prow"), "pcol"),
            P("groups", ("prow", "pcol"), None),
            P("groups", None, None),
            P("groups", None, None),
            P("groups"),
        ),
        out_specs=(P("groups", ("prow", "pcol"), None), P("groups", None, None, None)),
        check_vma=False,
    )
```

```python
import functools

import jax
import jax.numpy as jnp
from jax import lax
from jax.experimental import pallas as pl
from jax.experimental.pallas import tpu as pltpu
from jax.sharding import PartitionSpec as P

BLK = 128
PIECES = 4
DIRECT = (0,)
ORDER = ()
MESH = pl.DeviceIdType.MESH


def split(x):
    high = x.astype(jnp.bfloat16)
    return high, (x - high.astype(jnp.float32)).astype(jnp.bfloat16)


def product(a, b):
    dot = functools.partial(jnp.dot, preferred_element_type=jnp.float32)
    return dot(a[0], b[0]) + (dot(a[0], b[1]) + dot(a[1], b[0]))


def pair_at(first, second):
    return second * (second + 1) // 2 + first


def log2(n):
    return n.bit_length() - 1


class Plan:
    def __init__(self, n_prow, count, width):
        self.bits = log2(n_prow)
        self.blocks = [(first, node) for node in reversed(range(count)) for first in range(node + 1)]
        self.chunks = range(len(self.blocks))
        self.base = [pair_at(*block) * width for block in self.blocks]
        self.width = width
        self.piece = width // n_prow
        self.rows = len(self.blocks) * width

    def half(self, bit):
        return self.width // 2 ** (bit + 1)


def kernel(
    n_prow, n_pcol, plan, readers_ref, a_hbm, f_hbm, win_hbm, diag_hbm, panels_hbm, pairs_hbm,
    a_ref, f_ref, win_ref, diag_ref, v_ref, ath_ref, atl_ref, vh_ref, vl_ref,
    wh_ref, wl_ref, dh_ref, dl_ref, x_ref, s_ref, panel_ref,
    line_ref, turn_ref, y_ref, sum_ref, final_ref, fold_ref, middle_ref, direct_ref,
    load_sem, panel_sem, pairs_sem, line_send, line_recv,
    turn_send, turn_recv, y_send, y_recv, w_send, w_recv, back_send, back_recv, z_send, z_recv, direct_send, direct_recv,
    *more_refs,
):
    loads = [
        pltpu.make_async_copy(source, target, load_sem.at[at])
        for at, (source, target) in enumerate(
            [(f_hbm, f_ref), (a_hbm, a_ref), (diag_hbm, diag_ref), (win_hbm, win_ref)]
        )
    ]
    for load in loads:
        load.start()
    count, fine, width = f_ref.shape
    per_column = n_prow // n_pcol
    quarter = fine // PIECES
    bits = log2(n_prow)
    turn_in = more_refs[:bits]
    half_refs = more_refs[bits:]
    p = lax.axis_index("prow")
    z = lax.axis_index("pcol")
    order = list(reversed(range(count)))
    chunks_of = {node: [c for c in plan.chunks if plan.blocks[c][1] == node] for node in order}

    barrier = pltpu.get_barrier_semaphore()

    def greet(dest):
        pl.semaphore_signal(barrier, inc=1, device_id=dest, device_id_type=MESH)

    @pl.when(z > 0)
    def _():
        greet({"prow": p, "pcol": z - 1})

    @pl.when(z < n_pcol - 1)
    def _():
        greet({"prow": p, "pcol": z + 1})

    for bit in range(bits):
        greet({"prow": p + (1 - (p // 2**bit) % 2 * 2) * 2**bit, "pcol": z})
    greeted = bits + jnp.where(z > 0, 1, 0) + jnp.where(z < n_pcol - 1, 1, 0)

    reader = readers_ref[(p * n_pcol + z) * fine // BLK]
    masks = [jnp.where(reader <= node, 1.0, 0.0).astype(jnp.float32) for node in range(count)]

    def rows(start, size):
        return pl.ds(start if isinstance(start, int) else pl.multiple_of(start, 8), size)

    share = v_ref.shape[1] - fine
    unit_row = lax.broadcasted_iota(jnp.int32, (share, width), 0) + (p * n_pcol + z) * share
    unit_col = lax.broadcasted_iota(jnp.int32, (share, width), 1)

    def win_at(first, second):
        at = second * (second - 1) // 2 + first
        return wh_ref[at], wl_ref[at]

    def diag_at(node):
        return dh_ref[node], dl_ref[node]

    def split_factors():
        loads[2].wait()
        loads[3].wait()
        for node in range(count):
            dh_ref[node], dl_ref[node] = split(diag_ref[node])
        for at in range(win_ref.shape[0]):
            wh_ref[at], wl_ref[at] = split(win_ref[at])

    def local_v(node):
        units = jnp.where(unit_row == unit_col + node * width, 1.0, 0.0).astype(jnp.float32)
        total = jnp.concatenate([f_ref[node], units], axis=0)
        for other in range(node + 1, count):
            total = total - product(split(v_ref[other]), win_at(node, other))
        v = product(split(total), diag_at(node))
        v_ref[node] = v
        vh_ref[node], vl_ref[node] = split(v.T)

    def before_x(node):
        total = jnp.zeros((fine, width), jnp.float32)
        for other in range(node + 1, count):
            total = total + product(split(x_ref[other]), win_at(node, other))
        s_ref[node] = total

    def panel_copy(node):
        return pltpu.make_async_copy(panel_ref.at[node], panels_hbm.at[node], panel_sem.at[node])

    def window_part(node, y):
        x = product(split(y - s_ref[node]), diag_at(node))
        x_ref[node] = x
        ends = split(jnp.concatenate([x, v_ref[node, pl.ds(fine, share)]], axis=0))
        for other in range(node + 1):
            sum_ref[pl.ds(pair_at(other, node) * width, width)] = product((vh_ref[other], vl_ref[other]), ends)
        panel_ref[node] = -x * masks[node]
        panel_copy(node).start()

    middle = n_pcol // 2
    lower = z < middle
    beyond = jnp.where(lower, middle, middle - 1)
    toward = jnp.where(lower, z + 1, z - 1)
    outward = jnp.where(lower, z - 1, z + 1)
    depth = jnp.where(lower, z, n_pcol - 1 - z)
    relays = depth == middle - 1

    def line_copy(node, origin, dest, sem):
        return pltpu.make_async_remote_copy(
            src_ref=line_ref.at[node, origin],
            dst_ref=line_ref.at[node, origin],
            send_sem=sem,
            recv_sem=line_recv.at[node, origin],
            device_id={"prow": p, "pcol": dest},
            device_id_type=MESH,
        )

    def line_side(side, back):
        return z - back if side == 0 else z + back

    def line_sends(side, hop):
        if side == 0:
            return jnp.logical_and(z >= hop, z < n_pcol - 1)
        return jnp.logical_and(z + hop < n_pcol, z > 0)

    def line_gets(side, hop):
        return z - 1 - hop >= 0 if side == 0 else z + 1 + hop < n_pcol

    def line_step(node, hop):
        for side in (0, 1):
            if hop > 0:
                @pl.when(line_gets(side, hop - 1))
                def _():
                    line_copy(node, line_side(side, hop), line_side(side, 1), line_send.at[node, side, hop - 1]).wait_recv()

            if hop < n_pcol - 1:
                @pl.when(line_sends(side, hop))
                def _():
                    line_copy(node, line_side(side, hop), line_side(side, -1), line_send.at[node, side, hop]).start()

    def line_finish(node):
        for hop in range(n_pcol - 1):
            for side in (0, 1):
                @pl.when(line_sends(side, hop))
                def _():
                    line_copy(node, line_side(side, hop), line_side(side, -1), line_send.at[node, side, hop]).wait_send()

    def split_turned():
        loads[1].wait()
        turned = split(a_ref[...].T)
        for group in range(n_prow // PIECES):
            for owner in range(PIECES):
                for chunk in range(PIECES):
                    at = (group * PIECES + owner) * fine + chunk * quarter
                    to = (group * PIECES + chunk) * fine + owner * quarter
                    ath_ref[pl.ds(to, quarter)] = turned[0][at : at + quarter]
                    atl_ref[pl.ds(to, quarter)] = turned[1][at : at + quarter]

    turn_starts = [0]
    for bit in range(bits):
        turn_starts.append(turn_starts[bit] + (p // 2**bit) % 2 * (n_prow // 2 ** (bit + 1)))
    slot = turn_starts[bits]

    def mate(axis, bit):
        if axis == "prow":
            return {"prow": p + (1 - (p // 2**bit) % 2 * 2) * 2**bit, "pcol": z}
        return {"prow": p, "pcol": z + (1 - (z // 2**bit) % 2 * 2) * 2**bit}

    def turn_copy(node, bit):
        half = n_prow // 2 ** (bit + 1)
        away = turn_starts[bit] + (1 - (p // 2**bit) % 2) * half
        return pltpu.make_async_remote_copy(
            src_ref=turn_ref.at[node, pl.ds(away, half)],
            dst_ref=turn_in[bit].at[node],
            send_sem=turn_send.at[node, bit],
            recv_sem=turn_recv.at[node, bit],
            device_id=mate("prow", bit),
            device_id_type=MESH,
        )

    def turn_multiply(node):
        gathered = line_ref[node].reshape(a_ref.shape[0], width)
        result = product((ath_ref[...], atl_ref[...]), split(gathered))
        turn_ref[node] = result.reshape(n_prow, PIECES, quarter, width)
        turn_copy(node, 0).start()

    def y_copy(node, owner):
        place = slot // PIECES * PIECES + owner
        return pltpu.make_async_remote_copy(
            src_ref=turn_ref.at[node, slot, owner],
            dst_ref=y_ref.at[node, slot % PIECES],
            send_sem=y_send.at[node, owner],
            recv_sem=y_recv.at[node],
            device_id={"prow": z * per_column + place // n_pcol, "pcol": place % n_pcol},
            device_id_type=MESH,
        )

    def y_mine(owner):
        place = slot // PIECES * PIECES + owner
        return jnp.logical_and(z * per_column + place // n_pcol == p, place % n_pcol == z)

    def turn_step(node, bit):
        turn_copy(node, bit).wait_recv()
        mine = pl.ds(turn_starts[bit + 1], n_prow // 2 ** (bit + 1))
        turn_ref[node, mine] += turn_in[bit][node]
        if bit + 1 < bits:
            turn_copy(node, bit + 1).start()
            return
        for owner in range(PIECES):
            @pl.when(y_mine(owner))
            def _():
                pltpu.make_async_copy(
                    turn_ref.at[node, slot, owner], y_ref.at[node, slot % PIECES], y_recv.at[node]
                ).start()

            @pl.when(jnp.logical_not(y_mine(owner)))
            def _():
                y_copy(node, owner).start()

    def y_end(node):
        pltpu.make_async_copy(y_ref.at[node], y_ref.at[node], y_recv.at[node]).wait()

    def turn_finish(node):
        for bit in range(bits):
            turn_copy(node, bit).wait_send()
        for owner in range(PIECES):
            @pl.when(jnp.logical_not(y_mine(owner)))
            def _():
                y_copy(node, owner).wait_send()

    starts = [0]
    for bit in range(bits):
        starts.append(starts[bit] + (p // 2**bit) % 2 * plan.half(bit))

    def piece_rows(chunk):
        return rows(plan.base[chunk] + starts[bits], plan.piece)

    def chunk_rows(chunk, size):
        return pl.ds(chunk * size, size)

    def w_copy(chunk, bit):
        half = plan.half(bit)
        away = plan.base[chunk] + starts[bit] + (1 - (p // 2**bit) % 2) * half
        return pltpu.make_async_remote_copy(
            src_ref=sum_ref.at[rows(away, half)],
            dst_ref=half_refs[bit].at[chunk_rows(chunk, half)],
            send_sem=w_send.at[chunk, bit],
            recv_sem=w_recv.at[chunk, bit],
            device_id=mate("prow", bit),
            device_id_type=MESH,
        )

    def z_copy(chunk, kind, dest):
        source_ref = final_ref if kind == 2 else sum_ref
        target_ref = (fold_ref, middle_ref)[kind].at[chunk_rows(chunk, plan.piece)] if kind < 2 else None
        return pltpu.make_async_remote_copy(
            src_ref=source_ref.at[piece_rows(chunk)],
            dst_ref=final_ref.at[piece_rows(chunk)] if kind == 2 else target_ref,
            send_sem=z_send.at[chunk, kind],
            recv_sem=z_recv.at[chunk, kind],
            device_id={"prow": p, "pcol": dest},
            device_id_type=MESH,
        )

    def back_copy(chunk, bit):
        part = rows(plan.base[chunk] + starts[bit + 1], plan.half(bit))
        return pltpu.make_async_remote_copy(
            src_ref=final_ref.at[part],
            dst_ref=final_ref.at[part],
            send_sem=back_send.at[chunk, bit],
            recv_sem=back_recv.at[chunk, bit],
            device_id=mate("prow", bit),
            device_id_type=MESH,
        )

    def pairs_copy(chunk):
        part = pl.ds(plan.base[chunk], width)
        return pltpu.make_async_copy(final_ref.at[part], pairs_hbm.at[part], pairs_sem.at[chunk])

    members = n_prow // 2 * n_pcol
    member = p // 2 * n_pcol + z
    small = plan.half(0) // members
    direct = [c for c in plan.chunks if plan.blocks[c][1] in DIRECT and small % 8 == 0]

    def member_rows(chunk, at):
        return rows(plan.base[chunk] + starts[1] + at * small, small)

    def member_copy(chunk, kind, sender, dest):
        place = direct.index(chunk)
        if kind == 0:
            source_ref, target_ref = sum_ref.at[member_rows(chunk, dest)], direct_ref.at[place, sender]
        else:
            source_ref = target_ref = final_ref.at[member_rows(chunk, sender)]
        return pltpu.make_async_remote_copy(
            src_ref=source_ref,
            dst_ref=target_ref,
            send_sem=direct_send.at[place, kind, dest],
            recv_sem=direct_recv.at[place, kind, sender],
            device_id={"prow": dest // n_pcol * 2 + p % 2, "pcol": dest % n_pcol},
            device_id_type=MESH,
        )

    def members_but(run):
        for at in range(members):
            @pl.when(member != at)
            def _():
                run(at)

    def direct_start(chunk):
        w_copy(chunk, 0).wait_recv()
        half = plan.half(0)
        mine = rows(plan.base[chunk] + starts[1], half)
        sum_ref[mine] += half_refs[0][chunk_rows(chunk, half)]
        members_but(lambda at: member_copy(chunk, 0, member, at).start())

    def direct_sum(chunk):
        place = direct.index(chunk)
        direct_ref[place, member] = sum_ref[member_rows(chunk, member)]
        members_but(lambda at: member_copy(chunk, 0, at, at).wait_recv())
        total = direct_ref[place, 0]
        for at in range(1, members):
            total = total + direct_ref[place, at]
        final_ref[member_rows(chunk, member)] = total
        members_but(lambda at: member_copy(chunk, 1, member, at).start())

    def direct_end(chunk):
        members_but(lambda at: member_copy(chunk, 1, at, at).wait_recv())
        back_copy(chunk, 0).start()

    def direct_finish(chunk):
        w_copy(chunk, 0).wait_send()
        back_copy(chunk, 0).wait_send()
        for kind in (0, 1):
            members_but(lambda at: member_copy(chunk, kind, member, at).wait_send())
        pairs_copy(chunk).wait()

    def inward(chunk):
        @pl.when(depth < middle - 1)
        def _():
            z_copy(chunk, 0, toward).start()

        @pl.when(relays)
        def _():
            z_copy(chunk, 1, toward).start()

    def w_step(chunk, bit):
        w_copy(chunk, bit).wait_recv()
        half = plan.half(bit)
        mine = rows(plan.base[chunk] + starts[bit + 1], half)
        sum_ref[mine] += half_refs[bit][chunk_rows(chunk, half)]
        if bit + 1 < bits:
            w_copy(chunk, bit + 1).start()
        else:
            @pl.when(depth == 0)
            def _():
                inward(chunk)

    def fold_step(chunk, step):
        @pl.when(depth == step)
        def _():
            z_copy(chunk, 0, outward).wait_recv()
            sum_ref[piece_rows(chunk)] += fold_ref[chunk_rows(chunk, plan.piece)]
            inward(chunk)

    def outgoing(chunk):
        @pl.when(depth > 0)
        def _():
            z_copy(chunk, 2, outward).start()

        back_copy(chunk, bits - 1).start()

    def middle_step(chunk):
        @pl.when(relays)
        def _():
            z_copy(chunk, 1, toward).wait_recv()
            final_ref[piece_rows(chunk)] = sum_ref[piece_rows(chunk)] + middle_ref[chunk_rows(chunk, plan.piece)]
            outgoing(chunk)

    def unfold_step(chunk, step):
        @pl.when(depth == step)
        def _():
            z_copy(chunk, 2, toward).wait_recv()
            outgoing(chunk)

    def back_step(chunk, bit):
        back_copy(chunk, bit).wait_recv()
        if bit > 0:
            back_copy(chunk, bit - 1).start()
        else:
            pairs_copy(chunk).start()

    def window_finish(chunk):
        for bit in range(bits):
            w_copy(chunk, bit).wait_send()
            back_copy(chunk, bit).wait_send()

        @pl.when(depth < middle - 1)
        def _():
            z_copy(chunk, 0, toward).wait_send()

        @pl.when(relays)
        def _():
            z_copy(chunk, 1, toward).wait_send()

        @pl.when(depth > 0)
        def _():
            z_copy(chunk, 2, outward).wait_send()

        pairs_copy(chunk).wait()

    def close(node):
        window_part(node, y_ref[node].reshape(fine, width))
        for chunk in chunks_of[node]:
            w_copy(chunk, 0).start()

    def prepare(node):
        f_ref[node] = f_ref[node] * masks[node]
        line_ref[node, z] = f_ref[node]

    stages, due = {}, {}

    def at(time, name, run, *args):
        stages[name] = functools.partial(run, *args)
        due[name] = (time, len(due))

    at(0.0, ("bar",), pl.semaphore_wait, barrier, greeted)
    for node in order[1:]:
        at(0.2, ("p", node), prepare, node)
    at(0.3, ("st",), split_turned)
    at(1.0, ("sf",), split_factors)
    latest = 0.0
    for turn, node in enumerate(order):
        at(12.0 + 2.0 * turn, ("v", node), local_v, node)
        start = 7.5 * turn
        hops = n_pcol - 1
        at(0.1 + start, ("l", node, 0), line_step, node, 0)
        for hop in range(1, hops + 1):
            at(0.1 + start + 5.0 * hop, ("l", node, hop), line_step, node, hop)
        done = 0.2 + start + 5.0 * hops
        at(done, ("tm", node), turn_multiply, node)
        for bit in range(bits):
            done += 2.0 if bit == 0 else 5.0
            at(done, ("t", node, bit), turn_step, node, bit)
        latest = max(done + 5.0, latest + 2.0)
        at(latest - 1.0, ("b", node), before_x, node)
        at(latest, ("y", node), y_end, node)
        at(latest, ("x", node), close, node)
        for turn_w, chunk in enumerate(chunks_of[node]):
            time = latest + 2.0 * turn_w
            if chunk in direct:
                at(time + 2.0, ("w", chunk, 0), direct_start, chunk)
                at(time + 8.0, ("d", chunk, 0), direct_sum, chunk)
                at(time + 14.0, ("d", chunk, 1), direct_end, chunk)
                at(time + 16.0, ("k", chunk, 0), back_step, chunk, 0)
                continue
            for bit in range(bits):
                time += 2.0 if bit == 0 else 4.0
                at(time, ("w", chunk, bit), w_step, chunk, bit)
            for step in range(1, middle):
                time += 4.0
                at(time, ("w", chunk, bits + step - 1), fold_step, chunk, step)
            time += 4.0
            at(time, ("w", chunk, bits + middle - 1), middle_step, chunk)
            for step in reversed(range(middle - 1)):
                time += 4.0
                at(time, ("k", chunk, bits + step), unfold_step, chunk, step)
            for bit in reversed(range(bits)):
                time += 4.0 if bit else 2.0
                at(time, ("k", chunk, bit), back_step, chunk, bit)

    sequence = ORDER if set(ORDER) == set(stages) else sorted(stages, key=due.get)
    loads[0].wait()
    prepare(order[0])
    for name in sequence:
        stages[name]()
    for node in order:
        line_finish(node)
        turn_finish(node)
        panel_copy(node).wait()
    for chunk in plan.chunks:
        (direct_finish if chunk in direct else window_finish)(chunk)


def assemble_kernel(panels_in, pairs_in, panels_out, window_out, panel_ref, pairs_ref, turned_ref, in_sem, out_sem):
    count, _, width = panels_in.shape
    into = pltpu.make_async_copy(panels_in, panel_ref, in_sem.at[0])
    into.start()
    order = [(first, second) for second in reversed(range(count)) for first in range(second + 1)]

    def load(first, second):
        at = pair_at(first, second)
        return pltpu.make_async_copy(pairs_in.at[pl.ds(at * width, width)], pairs_ref.at[at], in_sem.at[1 + at])

    for first, second in order:
        load(first, second).start()
    stores = []
    for first, second in order:
        at = pair_at(first, second)
        load(first, second).wait()
        stores.append(pltpu.make_async_copy(pairs_ref.at[at], window_out.at[first, second], out_sem.at[1 + len(stores)]))
        stores[-1].start()
        if first != second:
            turned_ref[at] = pairs_ref[at].T
            stores.append(
                pltpu.make_async_copy(turned_ref.at[at], window_out.at[second, first], out_sem.at[1 + len(stores)])
            )
            stores[-1].start()
    into.wait()
    stores.append(pltpu.make_async_copy(panel_ref, panels_out, out_sem.at[0]))
    stores[-1].start()
    for store in stores:
        store.wait()


def sweep(n_prow, n_pcol, readers, anc_inverse, anc_factor, win_factor, diag_inverse):
    count, fine, width = anc_factor.shape
    pairs = count * (count + 1) // 2
    share = count * width // (n_prow * n_pcol)
    bits = log2(n_prow)
    quarter = fine // PIECES
    plan = Plan(n_prow, count, width)
    chunks = len(plan.chunks)
    members = n_prow // 2 * n_pcol
    block_rows, block_cols = anc_inverse.shape
    hbm = pl.BlockSpec(memory_space=pltpu.HBM)
    operands = (anc_inverse, anc_factor, win_factor, diag_inverse)
    f32, b16 = jnp.float32, jnp.bfloat16
    dma = pltpu.SemaphoreType.DMA
    panels, blocks = pl.pallas_call(
        functools.partial(kernel, n_prow, n_pcol, plan),
        out_shape=(
            jax.ShapeDtypeStruct((count, fine, width), f32),
            jax.ShapeDtypeStruct((pairs * width, width), f32),
        ),
        in_specs=[pl.BlockSpec(memory_space=pltpu.SMEM)] + [hbm] * 4,
        out_specs=(hbm, hbm),
        scratch_shapes=[pltpu.VMEM(operand.shape, f32) for operand in operands]
        + [
            pltpu.VMEM((count, fine + share, width), f32),
            pltpu.VMEM((block_cols, block_rows), b16),
            pltpu.VMEM((block_cols, block_rows), b16),
            pltpu.VMEM((count, width, fine + share), b16),
            pltpu.VMEM((count, width, fine + share), b16),
            pltpu.VMEM(win_factor.shape, b16),
            pltpu.VMEM(win_factor.shape, b16),
            pltpu.VMEM(diag_inverse.shape, b16),
            pltpu.VMEM(diag_inverse.shape, b16),
            pltpu.VMEM((count, fine, width), f32),
            pltpu.VMEM((count, fine, width), f32),
            pltpu.VMEM((count, fine, width), f32),
            pltpu.VMEM((count, n_pcol, fine, width), f32),
            pltpu.VMEM((count, n_prow, PIECES, quarter, width), f32),
            pltpu.VMEM((count, PIECES, quarter, width), f32),
            pltpu.VMEM((plan.rows, width), f32),
            pltpu.VMEM((plan.rows, width), f32),
            pltpu.VMEM((chunks * plan.piece, width), f32),
            pltpu.VMEM((chunks * plan.piece, width), f32),
            pltpu.VMEM((sum(DIRECT) + len(DIRECT), members, max(8, width // 2 // members), width), f32),
            dma((len(operands),)),
            dma((count,)),
            dma((chunks,)),
            dma((count, 2, n_pcol)),
            dma((count, n_pcol)),
            dma((count, bits)),
            dma((count, bits)),
            dma((count, PIECES)),
            dma((count,)),
            dma((chunks, bits)),
            dma((chunks, bits)),
            dma((chunks, bits)),
            dma((chunks, bits)),
            dma((chunks, 3)),
            dma((chunks, 3)),
            dma((sum(DIRECT) + len(DIRECT), 2, members)),
            dma((sum(DIRECT) + len(DIRECT), 2, members)),
        ]
        + [pltpu.VMEM((count, n_prow // 2 ** (bit + 1), PIECES, quarter, width), f32) for bit in range(bits)]
        + [pltpu.VMEM((chunks * plan.half(bit), width), f32) for bit in range(bits)],
        compiler_params=pltpu.CompilerParams(
            collective_id=0, has_side_effects=True, vmem_limit_bytes=58 * 2**20
        ),
    )(readers, *operands)
    return pl.pallas_call(
        assemble_kernel,
        out_shape=(
            jax.ShapeDtypeStruct((count, fine, width), f32),
            jax.ShapeDtypeStruct((count, count, width, width), f32),
        ),
        in_specs=[hbm, hbm],
        out_specs=(hbm, hbm),
        scratch_shapes=[
            pltpu.VMEM((count, fine, width), f32),
            pltpu.VMEM((pairs, width, width), f32),
            pltpu.VMEM((pairs, width, width), f32),
            dma((1 + pairs,)),
            dma((1 + count * count,)),
        ],
        compiler_params=pltpu.CompilerParams(vmem_limit_bytes=60 * 2**20),
    )(panels, blocks)


def per_device(anc_inverse, anc_factor, win_factor, diag_inverse, first_reader):
    n_prow = lax.axis_size("prow")
    n_pcol = lax.axis_size("pcol")
    return sweep(n_prow, n_pcol, first_reader, anc_inverse, anc_factor, win_factor, diag_inverse)


def solution(mesh):
    return jax.shard_map(
        per_device,
        mesh=mesh,
        in_specs=(
            P(("groups", "prow"), "pcol"),
            P("groups", ("prow", "pcol"), None),
            P("groups", None, None),
            P("groups", None, None),
            P("groups"),
        ),
        out_specs=(P("groups", ("prow", "pcol"), None), P("groups", None, None, None)),
        check_vma=False,
    )
```
